32 devices in a mesh: dp: 8 (over y, x, core), mp: 4 (over z).
Axes of the slice: x: 2, y: 2, z: 4, core: 2. Of those that a mesh axis runs over, the one named last changes fastest.
Arguments:
- hidden_in: bfloat16 [32, 512, 1024], P('dp', 'mp'), may hold values from -6 to 6
- lengths: int32 [32], P('dp'), may hold values from 128 to 512, as said below
- separators: int32 [32], P('dp'), may hold values from 32 to 383, as said below
- seg_table: float32 [2, 1024], replicated, may hold values from -3 to 3
- query_key_value_weight: bfloat16 [1024, 3, 1024], P('dp', None, 'mp'), may hold values from -0.25 to 0.25
- output_weight: bfloat16 [1024, 1024], P('dp', 'mp'), may hold values from -1.5 to 1.5
- up_weight: bfloat16 [1024, 4096], P('dp', 'mp'), may hold values from -0.1875 to 0.1875
- down_weight: bfloat16 [1024, 4096], P('dp', 'mp'), may hold values from -0.09375 to 0.09375
- bias_q: float32 [1024], replicated, may hold values from -2 to 2
- bias_v: float32 [1024], replicated, may hold values from -0.3 to 0.3
- bias_out: float32 [1024], replicated, may hold values from -2 to 2
- expand_bias: float32 [4096], replicated, may hold values from -2 to 2
- bias_down: float32 [1024], replicated, may hold values from -2 to 2
- gain_attn: float32 [1024], replicated, may hold values from 0.25 to 1.75
- shift_attn: float32 [1024], replicated, may hold values from -2 to 2
- gain_ffn: float32 [1024], replicated, may hold values from 0.25 to 1.75
- shift_ffn: float32 [1024], replicated, may hold values from -2 to 2
- cotangent: bfloat16 [32, 512, 1024], P('dp', 'mp'), may hold values from -8 to 8
Outputs:
- out_hidden: bfloat16 [32, 512, 1024], P('dp', 'mp')
- grad_hidden: bfloat16 [32, 512, 1024], P('dp', 'mp')
- grad_bias_q: float32 [1024], replicated
- grad_bias_v: float32 [1024], replicated
- grad_bias_out: float32 [1024], replicated
- grad_bias_up: float32 [4096], replicated
- grad_bias_down: float32 [1024], replicated
- grad_shift_attn: float32 [1024], replicated
- grad_shift_ffn: float32 [1024], replicated
The draws below stay inside these ranges and needn't reach their ends.
Inputs may be any that keep to these rules, and one draw needn't show every extreme that they name: `lengths`: every sequence whose index is a multiple of 4 has all 512 tokens, every one whose index is 2 more than a multiple of 4 has 128. `separators`: a separator lies between a quarter and three quarters of its sequence's length.
All inputs are finite; a program needn't handle non-finite values.
Results may differ from the reference program's by a relative error of at most 0.017.
Values may be sent and summed in bfloat16 or wider, within the bound.
A program may use at most 128 MiB of HBM per device.

```python
import math
import jax
import jax.numpy as jnp
from jax import lax

D = 1024
HEADS = 16
HEAD_DIM = 64
FF = 4096
SEQ_LEN = 512
SEQ_MB = 1
SEQS = 32
TOKENS = 16384


def lengths_and_separators(key):
    first_key, second_key = jax.random.split(jax.random.fold_in(key, 11))
    seq_index = jnp.arange(SEQS, dtype=jnp.int32)
    drawn_len = jax.random.randint(first_key, (SEQS,), SEQ_LEN // 4, SEQ_LEN + 1, dtype=jnp.int32)
    lengths = jnp.where(seq_index % 4 == 0, SEQ_LEN, jnp.where(seq_index % 4 == 2, SEQ_LEN // 4, drawn_len))
    offsets = jax.random.randint(second_key, (SEQS,), 0, 1048576, dtype=jnp.int32)
    separators = lengths // 4 + offsets % (lengths // 2)
    separators = jnp.where(seq_index % 8 == 0, SEQ_LEN // 4 + SEQ_LEN // 2 - 1, jnp.where(seq_index % 8 == 2, SEQ_LEN // 16, separators))
    return (lengths.astype(jnp.int32), separators.astype(jnp.int32))


def draw_lengths(key, part):
    return lengths_and_separators(key)[0]


def draw_separators(key, part):
    return lengths_and_separators(key)[1]


def draw_cotangent(key, part):
    noise_key, common_key = jax.random.split(jax.random.fold_in(key, 23))
    position = jnp.arange(SEQS, dtype=jnp.float32) / max(SEQS - 1, 1)
    noise = jnp.clip(jax.random.normal(noise_key, (SEQS, SEQ_LEN, D), jnp.float32), -5.0, 5.0)
    rising = jnp.exp(position * math.log(3.0))
    common = jnp.clip(jax.random.normal(common_key, (D,), jnp.float32), -4.0, 4.0) * 0.5
    values = jnp.clip(rising[:, None, None] * (noise + common), -8.0, 8.0)
    return values.astype(jnp.bfloat16)


def steps_of(own_key, extent, shards, low, top_value):
    level = 1.0
    for dim, shards_of in shards:
        draws = jax.random.uniform(jax.random.fold_in(jax.random.fold_in(own_key, 6), dim), (shards_of,), jnp.float32, low / len(shards), top_value / len(shards))
        level = level * jnp.repeat(jnp.exp(draws), extent[dim] // shards_of).reshape((-1,) + (1,) * (len(extent) - 1 - dim))
    return level


def gaussian(stream_key, shape, width, most, pieces=(), kind=jnp.bfloat16):
    level = steps_of(stream_key, shape, pieces, -0.22, 0.18) if pieces else 1.0
    values = jax.random.normal(stream_key, shape, jnp.float32) * width * level
    return jnp.minimum(jnp.maximum(values, -most), most).astype(kind)


def setup_inputs(seed: int = 0) -> dict:
    streams_of = jax.random.split(jax.random.key(seed), 19)
    return {
        "hidden_in": gaussian(streams_of[0], (SEQS, SEQ_LEN, D), 1.0, 6.0, ((0, 8), (1, 4))),
        "lengths": draw_lengths(jax.random.fold_in(streams_of[18], 71), 0),
        "separators": draw_separators(jax.random.fold_in(streams_of[18], 71), 0),
        "seg_table": gaussian(streams_of[3], (2, D), 0.5, 3.0, (), jnp.float32),
        "query_key_value_weight": gaussian(streams_of[4], (D, 3, D), (D // 2) ** -0.5, 0.25, ((0, 8), (2, 4))),
        "output_weight": gaussian(streams_of[5], (D, D), (max(D // 64, 1)) ** -0.5, 1.5, ((0, 8), (1, 4))),
        "up_weight": gaussian(streams_of[6], (D, FF), D ** -0.5, 0.1875, ((0, 8), (1, 4))),
        "down_weight": gaussian(streams_of[7], (D, FF), FF ** -0.5, 0.09375, ((0, 8), (1, 4))),
        "bias_q": gaussian(streams_of[8], (D,), 0.3, 2.0, (), jnp.float32),
        "bias_v": gaussian(streams_of[9], (D,), 0.04, 0.3, (), jnp.float32),
        "bias_out": gaussian(streams_of[10], (D,), 0.3, 2.0, (), jnp.float32),
        "expand_bias": gaussian(streams_of[11], (FF,), 0.3, 2.0, (), jnp.float32),
        "bias_down": gaussian(streams_of[12], (D,), 0.3, 2.0, (), jnp.float32),
        "gain_attn": jnp.clip(1.0 + 0.15 * jax.random.normal(streams_of[13], (D,), jnp.float32), 0.25, 1.75),
        "shift_attn": gaussian(streams_of[14], (D,), 0.3, 2.0, (), jnp.float32),
        "gain_ffn": jnp.clip(1.0 + 0.15 * jax.random.normal(streams_of[15], (D,), jnp.float32), 0.25, 1.75),
        "shift_ffn": gaussian(streams_of[16], (D,), 0.3, 2.0, (), jnp.float32),
        "cotangent": draw_cotangent(jax.random.fold_in(streams_of[18], 71), 0),
    }


EPS = 1e-12
PRECISE_MODE = lax.Precision.HIGHEST

@jax.custom_vjp
def reduced_precision(v):
    return lax.optimization_barrier(v.astype(jnp.bfloat16)).astype(jnp.float32)

@jax.custom_vjp
def reduced_backward(v):
    return v

def low_keep(v):
    return (reduced_precision(v), None)

def low_pass(kept, grad):
    return (grad,)

def back_keep(v):
    return (v, None)

def back_low(kept, grad):
    return (reduced_precision(grad),)
reduced_precision.defvjp(low_keep, low_pass)
reduced_backward.defvjp(back_keep, back_low)

def layer_norm(values, gain, shift):
    center = values - lax.optimization_barrier(jnp.mean(values, axis=-1, keepdims=True))
    spread = lax.optimization_barrier(jnp.mean(center * center, axis=-1, keepdims=True))
    return center * lax.rsqrt(spread + EPS) * gain + shift

def block(hidden, seg_flag, key_valid, frozen, bias_q, bias_v, bias_out, expand_bias, bias_down, shift_attn, shift_ffn):
    query_key_value_weight, output_weight, up_weight, down_weight, seg_table, gain_attn, gain_ffn = frozen
    groups = hidden.shape[0]
    scale = 1.0 / math.sqrt(HEAD_DIM)
    embedded_tokens = hidden + seg_table[0] + seg_flag[..., None] * (seg_table[1] - seg_table[0])
    projected_rows = jnp.einsum('tzo,ogv->tzgv', reduced_precision(embedded_tokens), query_key_value_weight, precision=PRECISE_MODE)
    queries = reduced_precision(reduced_backward((projected_rows[:, :, 0] + bias_q) * scale)).reshape(groups, SEQ_LEN, HEADS, HEAD_DIM)
    keyset = reduced_precision(reduced_backward(projected_rows[:, :, 1])).reshape(groups, SEQ_LEN, HEADS, HEAD_DIM)
    value_rows = reduced_precision(reduced_backward(projected_rows[:, :, 2] + bias_v)).reshape(groups, SEQ_LEN, HEADS, HEAD_DIM)
    scores = jnp.einsum('sqhd,skhd->shqk', queries, keyset, precision=PRECISE_MODE)
    scores = reduced_backward(jnp.where(key_valid[:, None, None, :], scores, -1e+30))
    highest = lax.optimization_barrier(jnp.max(scores, axis=-1, keepdims=True))
    expanded = jnp.exp(scores - highest)
    probs = expanded / lax.optimization_barrier(jnp.sum(expanded, axis=-1, keepdims=True))
    context_rows = jnp.einsum('shqk,skhd->sqhd', reduced_precision(probs), value_rows, precision=PRECISE_MODE).reshape(groups, SEQ_LEN, D)
    context_rows = reduced_precision(reduced_backward(context_rows))
    attended_rows = reduced_backward(jnp.einsum('mqg,ag->mqa', context_rows, output_weight, precision=PRECISE_MODE))
    normalized_rows = layer_norm(embedded_tokens + attended_rows + bias_out, gain_attn, shift_attn)
    inner_activation = reduced_backward(jnp.einsum('twv,ve->twe', reduced_precision(normalized_rows), up_weight, precision=PRECISE_MODE) + expand_bias)
    active_units = reduced_precision(jax.nn.gelu(inner_activation, approximate=False))
    feedforward_output = reduced_backward(jnp.einsum('jrx,vx->jrv', active_units, down_weight, precision=PRECISE_MODE))
    return layer_norm(normalized_rows + feedforward_output + bias_down, gain_ffn, shift_ffn)

def reference(hidden_in, lengths, separators, seg_table, query_key_value_weight, output_weight, up_weight, down_weight, bias_q, bias_v, bias_out, expand_bias, bias_down, gain_attn, shift_attn, gain_ffn, shift_ffn, cotangent):
    groups = SEQS // SEQ_MB
    frozen = (query_key_value_weight.astype(jnp.float32), output_weight.astype(jnp.float32), up_weight.astype(jnp.float32), down_weight.astype(jnp.float32), seg_table.astype(jnp.float32), gain_attn, gain_ffn)
    positions = jnp.arange(SEQ_LEN, dtype=jnp.int32)
    seg_flag = (positions[None, :] > separators[:, None]).astype(jnp.float32)
    key_valid = positions[None, :] < lengths[:, None]

    def one_group(carry, slices):
        hidden, flags, valid, grad_out = slices

        def forward(hidden_value, b_q, b_v, b_out, b_up, b_down, s_attn, s_ffn):
            return block(hidden_value, flags, valid, frozen, b_q, b_v, b_out, b_up, b_down, s_attn, s_ffn)
        result, pullback = jax.vjp(forward, hidden, bias_q, bias_v, bias_out, expand_bias, bias_down, shift_attn, shift_ffn)
        grads = pullback(grad_out)
        carry = tuple((held + fresh for held, fresh in zip(carry, grads[1:])))
        return (carry, (result.astype(jnp.bfloat16), grads[0].astype(jnp.bfloat16)))
    inputs = (hidden_in.astype(jnp.float32).reshape(groups, SEQ_MB, SEQ_LEN, D), seg_flag.reshape(groups, SEQ_MB, SEQ_LEN), key_valid.reshape(groups, SEQ_MB, SEQ_LEN), cotangent.astype(jnp.float32).reshape(groups, SEQ_MB, SEQ_LEN, D))
    start = (jnp.zeros((D,), jnp.float32), jnp.zeros((D,), jnp.float32), jnp.zeros((D,), jnp.float32), jnp.zeros((FF,), jnp.float32), jnp.zeros((D,), jnp.float32), jnp.zeros((D,), jnp.float32), jnp.zeros((D,), jnp.float32))
    totals, (outputs, input_grads) = lax.scan(one_group, start, inputs)
    factor = 1.0 / TOKENS
    return (outputs.reshape(SEQS, SEQ_LEN, D), input_grads.reshape(SEQS, SEQ_LEN, D), totals[0] * factor, totals[1] * factor, totals[2] * factor, totals[3] * factor, totals[4] * factor, totals[5] * factor, totals[6] * factor)
```

```python
import math

import jax
import jax.numpy as jnp
from jax import lax
from jax.sharding import PartitionSpec as P

HEAD_DIM = 64
EPS = 1e-12
F32 = jnp.float32
BF16 = jnp.bfloat16


def norm_parts(values, gain, shift):
    center = values - jnp.mean(values, axis=-1, keepdims=True)
    inverse = lax.rsqrt(jnp.mean(center * center, axis=-1, keepdims=True) + EPS)
    normal = center * inverse
    return normal * gain + shift, normal, inverse


def norm_back(grad, normal, inverse, gain):
    scaled = grad * gain
    return inverse * (
        scaled
        - jnp.mean(scaled, axis=-1, keepdims=True)
        - normal * jnp.mean(scaled * normal, axis=-1, keepdims=True)
    )


def dot(a, b, dims):
    return lax.dot_general(a, b, (dims, ((), ())), preferred_element_type=F32)


def gather_whole(shard):
    rows = lax.all_gather(shard, "dp", axis=0, tiled=True)
    return lax.all_gather(rows, "mp", axis=rows.ndim - 1, tiled=True)


def on_device(
    hidden_in, lengths, separators, seg_table, query_key_value_weight, output_weight, up_weight, down_weight,
    bias_q, bias_v, bias_out, expand_bias, bias_down, gain_attn, shift_attn, gain_ffn, shift_ffn, cotangent,
):
    model_size = lax.axis_size("mp")
    model_index = lax.axis_index("mp")
    here = hidden_in.shape[0] // model_size

    def to_sequences(rows):
        return lax.all_to_all(rows, "mp", split_axis=0, concat_axis=1, tiled=True)

    def to_tokens(rows):
        return lax.all_to_all(rows, "mp", split_axis=1, concat_axis=0, tiled=True)

    hidden = to_sequences(hidden_in)
    grad_rows = to_sequences(cotangent)
    own = model_index * here
    length = lax.dynamic_slice_in_dim(lengths, own, here)
    separator = lax.dynamic_slice_in_dim(separators, own, here)
    wqkv, wo, wup, wdown = (gather_whole(w) for w in (query_key_value_weight, output_weight, up_weight, down_weight))
    seqs, seq_len, width = hidden.shape
    total_tokens = seqs * seq_len * model_size * lax.axis_size("dp")
    heads = width // HEAD_DIM
    scale = 1.0 / math.sqrt(HEAD_DIM)
    positions = jnp.arange(seq_len, dtype=jnp.int32)
    flag = (positions[None, :] > separator[:, None]).astype(F32)
    embedded = hidden.astype(F32) + seg_table[0] + flag[..., None] * (seg_table[1] - seg_table[0])
    low = embedded.astype(BF16)
    projected = jnp.einsum("tzo,ogv->gtzv", low, wqkv, preferred_element_type=F32)
    shape = (seqs, seq_len, heads, HEAD_DIM)
    queries = ((projected[0] + bias_q) * scale).astype(BF16).reshape(shape)
    keys = projected[1].astype(BF16).reshape(shape)
    values = (projected[2] + bias_v).astype(BF16).reshape(shape)
    scores = jnp.einsum("sqhd,skhd->shqk", queries, keys, preferred_element_type=F32)
    valid = positions[None, :] < length[:, None]
    scores = jnp.where(valid[:, None, None, :], scores, -1e30)
    expanded = jnp.exp(scores - jnp.max(scores, axis=-1, keepdims=True))
    probs = expanded / jnp.sum(expanded, axis=-1, keepdims=True)
    low_probs = probs.astype(BF16)
    context = jnp.einsum("shqk,skhd->sqhd", low_probs, values, preferred_element_type=F32)
    context = context.reshape(seqs, seq_len, width).astype(BF16)
    attended = jnp.einsum("mqg,ag->mqa", context, wo, preferred_element_type=F32)
    normed, normal_attn, inv_attn = norm_parts(embedded + attended + bias_out, gain_attn, shift_attn)
    inner = jnp.einsum("twv,ve->twe", normed.astype(BF16), wup, preferred_element_type=F32) + expand_bias
    cdf = 0.5 * (1.0 + lax.erf(inner * math.sqrt(0.5)))
    slope = cdf + inner * jnp.exp(-0.5 * inner * inner) * (1.0 / math.sqrt(2.0 * math.pi))
    active = (inner * cdf).astype(BF16)
    ffn_out = jnp.einsum("jrx,vx->jrv", active, wdown, preferred_element_type=F32)
    result, normal_ffn, inv_ffn = norm_parts(normed + ffn_out + bias_down, gain_ffn, shift_ffn)
    out_hidden = to_tokens(result.astype(BF16))
    dy = grad_rows.astype(F32)
    grad_mid = norm_back(dy, normal_ffn, inv_ffn, gain_ffn)
    grad_active = jnp.einsum("twv,ve->twe", grad_mid.astype(BF16), wdown, preferred_element_type=F32)
    grad_inner = (grad_active * slope).astype(BF16)
    grad_normed = grad_mid + jnp.einsum("jrx,vx->jrv", grad_inner, wup, preferred_element_type=F32)
    grad_first = norm_back(grad_normed, normal_attn, inv_attn, gain_attn)
    grad_context = jnp.einsum("fox,xn->fon", grad_first.astype(BF16), wo, preferred_element_type=F32)
    grad_context = grad_context.astype(BF16).reshape(shape)
    grad_probs = jnp.einsum("sqhd,skhd->shqk", grad_context, values, preferred_element_type=F32)
    grad_values = jnp.einsum("shqk,sqhd->skhd", low_probs, grad_context, preferred_element_type=F32).astype(BF16)
    inner_sum = jnp.sum(probs * grad_probs, axis=-1, keepdims=True)
    grad_scores = (probs * (grad_probs - inner_sum)).astype(BF16)
    grad_queries = jnp.einsum("shqk,skhd->sqhd", grad_scores, keys, preferred_element_type=F32).astype(BF16) * scale
    grad_keys = jnp.einsum("shqk,sqhd->skhd", grad_scores, queries, preferred_element_type=F32).astype(BF16)
    flat = (seqs, seq_len, width)
    grad_queries, grad_keys, grad_values = (g.reshape(flat) for g in (grad_queries, grad_keys, grad_values))
    stacked = jnp.stack([grad_queries, grad_keys, grad_values], axis=2)
    grad_embedded = grad_first + jnp.einsum("hgax,bax->hgb", stacked, wqkv, preferred_element_type=F32)
    grad_hidden = to_tokens(grad_embedded.astype(BF16))
    sums = tuple(
        jnp.sum(g.astype(F32), axis=(0, 1)) * (1.0 / total_tokens)
        for g in (grad_queries, grad_values, grad_first, grad_inner, grad_mid, grad_normed, dy)
    )
    return (out_hidden, grad_hidden) + lax.psum(sums, ("dp", "mp"))


def solution(mesh):
    rows = P("dp", "mp", None)
    frozen = P("dp", "mp")
    placed = (rows, P("dp"), P("dp"), P(), P("dp", None, "mp"), frozen, frozen, frozen) + (P(),) * 9 + (rows,)
    return jax.shard_map(on_device, mesh=mesh, in_specs=placed, out_specs=(rows, rows) + (P(),) * 7, check_vma=False)
```

```python
import functools
import math

import jax
import jax.numpy as jnp
from jax import lax
from jax.experimental import pallas as pl
from jax.experimental.pallas import tpu as pltpu
from jax.sharding import PartitionSpec as P

HEAD_DIM = 64
EPS = 1e-12
F32 = jnp.float32
BF16 = jnp.bfloat16
MESH = pl.DeviceIdType.MESH
ROWS = 64
NN = ((1,), (0,))
NT = ((1,), (1,))


def dot(a, b, dims=NN):
    return lax.dot_general(a, b, (dims, ((), ())), preferred_element_type=F32)


def snake(pos):
    high = pos // 2
    return 2 * high + (pos % 2 + high) % 2


def row_mean(x):
    return jnp.sum(x, axis=-1, keepdims=True) * (1.0 / x.shape[-1])


def step_kernel(
    shape, lens, seps, seg, bias_q, bias_v, bias_out, expand_bias, bias_down, gain_attn, shift_attn, gain_ffn,
    shift_ffn, hid, cot, wq_in, wo_in, wu_in, wd_in,
    out, grad, sum_q, sum_v, sum_out, sum_up, sum_down, sum_attn, sum_ffn,
    wq, wo, wu, wd, xh, ct, outb, low, qs, ks, vs, probs, normal, inverse, acc, act, slope, gctx,
    local_sem, ici_sem, sib_sem, send_sem, row_recv, row_send,
):
    dp, mp, seq, width, units = shape
    ring, half = dp // 2, dp // 4
    rb = width // dp
    cq = width // mp
    cu = units // mp
    hu = cu // 2
    tok = seq // mp
    heads = width // HEAD_DIM
    scale = 1.0 / math.sqrt(HEAD_DIM)
    d = lax.axis_index("dp")
    z = lax.axis_index("mp")
    core = d % 2
    pos = snake(d // 2)
    right = (2 * snake((pos + 1) % ring) + core, z)
    left = (2 * snake((pos + ring - 1) % ring) + core, z)
    sibling = (d + 1 - 2 * core, z)
    wholes = (wq, wo, wu, wd)
    shards = (wq_in, wo_in, wu_in, wd_in)

    def region(b, j, k, origin):
        zz = (z + mp - k) % mp
        rows = pl.ds(pl.multiple_of((2 * snake(origin) + core) * rb, rb), rb)
        if b == 0:
            return wq.at[:, rows, pl.ds(pl.multiple_of(zz * cq, 128), cq)]
        if b == 1:
            return wo.at[rows, pl.ds(pl.multiple_of(zz * cq, 128), cq)]
        return wholes[b].at[rows, pl.ds(pl.multiple_of(zz * cu + j * hu, 128), hu)]

    def own_shard(b, j):
        if b < 2:
            return shards[b]
        return shards[b].at[:, pl.ds(pl.multiple_of(j * hu, 128), hu)]

    def piece(b, j):
        return (0, 1, 2, 4)[b] + j

    def send(src, b, j, k, origin, way, target):
        zz = (z + mp - k) % mp
        dst = region(b, j, k, origin)
        recv = sib_sem.at[piece(b, j), zz] if way == 2 else ici_sem.at[piece(b, j), zz, origin]
        pltpu.make_async_remote_copy(
            src_ref=src, dst_ref=dst, send_sem=send_sem.at[b, way], recv_sem=recv, device_id=target, device_id_type=MESH
        ).start()

    def arrived(b, j, k, origin):
        zz = (z + mp - k) % mp
        ref = region(b, j, k, origin)
        pltpu.make_async_copy(ref, ref, ici_sem.at[piece(b, j), zz, origin]).wait()
        return ref

    def spread(src, b, j, k):
        send(src, b, j, k, pos, 0, right)
        send(src, b, j, k, pos, 1, left)
        send(src, b, j, k, pos, 2, sibling)

    def start_own(b, j):
        for hop in range(1, mp):
            there = (z + hop) % mp
            send_z(b, j, there)
        spread(own_shard(b, j), b, j, 0)

    def send_z(b, j, there):
        pltpu.make_async_remote_copy(
            src_ref=own_shard(b, j), dst_ref=region(b, j, 0, pos), send_sem=send_sem.at[b, 3],
            recv_sem=ici_sem.at[piece(b, j), z, pos], device_id=(d, there), device_id_type=MESH,
        ).start()

    def serve_column(b, j, k):
        spread(arrived(b, j, k, pos), b, j, k)

    def pick(cond, fn):
        if isinstance(cond, bool):
            if cond:
                fn()
        else:
            pl.when(cond)(fn)

    def serve_ring(b, j, k, dist):
        even, odd = k % 2 == 0, k % 2 == 1

        def from_left():
            origin = (pos + ring - dist) % ring
            ref = arrived(b, j, k, origin)
            if dist + 1 < half:
                send(ref, b, j, k, origin, 0, right)
            elif dist + 1 == half:
                pick(even, lambda: send(ref, b, j, k, origin, 0, right))
            send(ref, b, j, k, origin, 2, sibling)

        def from_right():
            origin = (pos + dist) % ring
            ref = arrived(b, j, k, origin)
            if dist + 1 < half:
                send(ref, b, j, k, origin, 1, left)
            elif dist + 1 == half:
                pick(odd, lambda: send(ref, b, j, k, origin, 1, left))
            send(ref, b, j, k, origin, 2, sibling)

        if dist < half:
            from_left()
            from_right()
        else:
            pick(even, from_left)
            pick(odd, from_right)

    def serve_item(b, j, k):
        pick(k > 0, lambda: serve_column(b, j, k))
        for dist in range(1, half + 1):
            serve_ring(b, j, k, dist)

    def sibling_done(b, j, k):
        zz = (z + mp - k) % mp
        if b == 0:
            ref = wq.at[:, pl.ds(0, width // 2), pl.ds(0, cq)]
        elif b == 1:
            ref = wo.at[pl.ds(0, width // 2), pl.ds(0, cq)]
        else:
            ref = wholes[b].at[pl.ds(0, width // 2), pl.ds(0, hu)]
        pltpu.make_async_copy(ref, ref, sib_sem.at[piece(b, j), zz]).wait()

    def tokens(ref, block):
        return ref.at[pl.ds(pl.multiple_of(block * tok, tok), tok), :]

    def own_local(b):
        zz = z
        rows = pl.ds(pl.multiple_of(d * rb, rb), rb)
        if b == 0:
            dst = wq.at[:, rows, pl.ds(pl.multiple_of(zz * cq, 128), cq)]
        elif b == 1:
            dst = wo.at[rows, pl.ds(pl.multiple_of(zz * cq, 128), cq)]
        else:
            dst = wholes[b].at[rows, pl.ds(pl.multiple_of(zz * cu, 128), cu)]
        return pltpu.make_async_copy(shards[b], dst, local_sem.at[b])

    barrier = pltpu.get_barrier_semaphore()
    partners = [sibling, right, left] + [(d, (z + hop) % mp) for hop in range(1, mp)]
    for target in partners:
        pl.semaphore_signal(barrier, inc=1, device_id=target, device_id_type=MESH)
    for b in range(4):
        own_local(b).start()
    own_hid = pltpu.make_async_copy(hid.at[z], tokens(xh, z), local_sem.at[4])
    own_cot = pltpu.make_async_copy(cot.at[z], tokens(ct, z), local_sem.at[5])
    own_hid.start()
    own_cot.start()
    pl.semaphore_wait(barrier, len(partners))

    def exchange_in(src, dst, which):
        for hop in range(1, mp):
            there = (z + hop) % mp
            pltpu.make_async_remote_copy(
                src_ref=src.at[there], dst_ref=tokens(dst, z), send_sem=row_send.at[which, there],
                recv_sem=row_recv.at[which, z], device_id=(d, there), device_id_type=MESH,
            ).start()

    def exchange_wait(src, dst, which):
        for hop in range(1, mp):
            there = (z + hop) % mp
            pltpu.make_async_copy(tokens(dst, there), tokens(dst, there), row_recv.at[which, there]).wait()

    def sends_wait(ref, which):
        for hop in range(1, mp):
            there = (z + hop) % mp
            pltpu.make_async_copy(ref, ref, row_send.at[which, there]).wait()

    start_own(0, 0)
    exchange_in(hid, xh, 0)
    start_own(1, 0)
    for b in (2, 3):
        for j in range(2):
            start_own(b, j)
    exchange_in(cot, ct, 1)

    for b in range(2):
        for k in range(mp):
            serve_item(b, 0, k)
    own_hid.wait()
    exchange_wait(hid, xh, 0)
    length = lens[z]
    separator = seps[z]
    seg0 = seg[0:1, :]
    seg_step = seg[1:2, :] - seg[0:1, :]

    def embed(rows, first):
        at = lax.broadcasted_iota(jnp.int32, (ROWS, 1), 0) + first
        flag = jnp.where(at > separator, 1.0, 0.0).astype(F32)
        return xh[rows, :].astype(F32) + seg0 + flag * seg_step

    @pl.loop(0, seq // ROWS)
    def _(i):
        first = pl.multiple_of(i * ROWS, ROWS)
        rows = pl.ds(first, ROWS)
        low[rows, :] = embed(rows, first).astype(BF16)

    own_local(0).wait()
    for k in range(mp):
        sibling_done(0, 0, k)

    tile = 256

    @pl.loop(0, width // tile)
    def _(i):
        cols = pl.ds(pl.multiple_of(i * tile, tile), tile)
        qs[:, cols] = ((dot(low[...], wq[0, :, cols]) + bias_q[:, cols]) * scale).astype(BF16)
        ks[:, cols] = dot(low[...], wq[1, :, cols]).astype(BF16)
        vs[:, cols] = (dot(low[...], wq[2, :, cols]) + bias_v[:, cols]).astype(BF16)

    pairs = heads // 2
    lane = lax.broadcasted_iota(jnp.int32, (seq, 2 * HEAD_DIM), 1)

    def half_of(x, hh):
        keep = lane < HEAD_DIM if hh == 0 else lane >= HEAD_DIM
        return jnp.where(keep, x, jnp.zeros_like(x))

    items = 2 * mp

    @pl.loop(0, pairs)
    def _(i):
        for part in range(max(1, items // pairs)):
            item = i * max(1, items // pairs) + part
            serve_item(2, item // mp, item % mp)
        cols = pl.ds(pl.multiple_of(i * 128, 128), 128)
        q2 = qs[:, cols]
        k2 = ks[:, cols]
        v2t = vs[:, cols].T
        ctxs = []
        for hh in range(2):
            st = dot(half_of(k2, hh), q2, NT)
            valid = lax.broadcasted_iota(jnp.int32, st.shape, 0) < length
            st = jnp.where(valid, st, -1e30)
            e = jnp.exp(st - jnp.max(st, axis=0, keepdims=True))
            p = (e * (1.0 / jnp.sum(e, axis=0, keepdims=True))).astype(BF16)
            probs[2 * i + hh] = p
            ctxs.append(dot(v2t[hh * HEAD_DIM:(hh + 1) * HEAD_DIM], p))
        low[:, cols] = jnp.concatenate(ctxs, axis=0).T.astype(BF16)

    own_local(1).wait()
    for k in range(mp):
        sibling_done(1, 0, k)

    @pl.loop(0, width // tile)
    def _(i):
        cols = pl.ds(pl.multiple_of(i * tile, tile), tile)
        acc[:, cols] = dot(low[...], wo[cols, :], NT)

    @pl.loop(0, seq // ROWS)
    def _(i):
        first = pl.multiple_of(i * ROWS, ROWS)
        rows = pl.ds(first, ROWS)
        x = embed(rows, first) + acc[rows, :] + bias_out[...]
        center = x - row_mean(x)
        inv = lax.rsqrt(row_mean(center * center) + EPS)
        norm = center * inv
        normal[rows, :] = norm
        inverse[rows, :] = jnp.broadcast_to(inv, (ROWS, 128))
        low[rows, :] = (norm * gain_attn[...] + shift_attn[...]).astype(BF16)
        acc[rows, :] = jnp.zeros((ROWS, width), F32)

    own_local(2).wait()
    for j in range(2):
        for k in range(mp):
            sibling_done(2, j, k)

    tiles = units // tile
    early = mp

    @pl.loop(0, tiles)
    def _(i):
        @pl.when(i % (tiles // early) == 0)
        def _():
            item = i // (tiles // early)
            serve_item(3, item // mp, item % mp)

        cols = pl.ds(pl.multiple_of(i * tile, tile), tile)
        inner = dot(low[...], wu[:, cols]) + expand_bias[:, cols]
        cdf = 0.5 * (1.0 + lax.erf(inner * math.sqrt(0.5)))
        act[:, cols] = (inner * cdf).astype(BF16)
        slope[:, cols] = (cdf + inner * (jnp.exp(-0.5 * inner * inner) * (1.0 / math.sqrt(2.0 * math.pi)))).astype(BF16)

    own_local(3).wait()

    @pl.loop(0, items)
    def _(i):
        @pl.when(i + early < items)
        def _():
            ahead = i + early
            serve_item(3, ahead // mp, ahead % mp)

        j = i // mp
        k = i % mp
        sibling_done(3, j, k)
        zz = (z + mp - k) % mp
        cols = pl.ds(pl.multiple_of(zz * cu + j * hu, 128), hu)

        @pl.loop(0, width // 512)
        def _(n):
            rows = pl.ds(pl.multiple_of(n * 512, 512), 512)
            acc[:, rows] += dot(act[:, cols], wd[rows, cols], NT)

    own_cot.wait()
    exchange_wait(cot, ct, 1)
    sum_ffn[...] = jnp.zeros_like(sum_ffn)
    sum_down[...] = jnp.zeros_like(sum_down)
    sum_attn[...] = jnp.zeros_like(sum_attn)
    sum_out[...] = jnp.zeros_like(sum_out)

    @pl.loop(0, seq // ROWS)
    def _(i):
        rows = pl.ds(pl.multiple_of(i * ROWS, ROWS), ROWS)
        x = normal[rows, :] * gain_attn[...] + shift_attn[...] + acc[rows, :] + bias_down[...]
        center = x - row_mean(x)
        inv = lax.rsqrt(row_mean(center * center) + EPS)
        norm = center * inv
        outb[rows, :] = (norm * gain_ffn[...] + shift_ffn[...]).astype(BF16)
        dy = ct[rows, :].astype(F32)
        e = dy * gain_ffn[...]
        g = inv * (e - row_mean(e) - norm * row_mean(e * norm))
        acc[rows, :] = g
        low[rows, :] = g.astype(BF16)
        sum_ffn[...] += jnp.sum(dy, axis=0, keepdims=True)
        sum_down[...] += jnp.sum(g, axis=0, keepdims=True)

    def push_out(buf, dst, which, there):
        pltpu.make_async_remote_copy(
            src_ref=tokens(buf, there), dst_ref=dst.at[z], send_sem=row_send.at[which, there],
            recv_sem=row_recv.at[which, z], device_id=(d, there), device_id_type=MESH,
        ).start()

    for hop in range(1, mp):
        push_out(outb, out, 2, (z + hop) % mp)
    keep_out = pltpu.make_async_copy(tokens(outb, z), out.at[z], local_sem.at[6])
    keep_out.start()

    @pl.loop(0, tiles)
    def _(i):
        cols = pl.ds(pl.multiple_of(i * tile, tile), tile)
        g = (dot(low[...], wd[:, cols]) * slope[:, cols].astype(F32)).astype(BF16)
        act[:, cols] = g
        sum_up[:, cols] = jnp.sum(g.astype(F32), axis=0, keepdims=True)

    @pl.loop(0, width // tile)
    def _(i):
        cols = pl.ds(pl.multiple_of(i * tile, tile), tile)
        acc[:, cols] += dot(act[...], wu[cols, :], NT)

    @pl.loop(0, seq // ROWS)
    def _(i):
        rows = pl.ds(pl.multiple_of(i * ROWS, ROWS), ROWS)
        g = acc[rows, :]
        norm = normal[rows, :]
        e = g * gain_attn[...]
        first = inverse[rows, 0:1] * (e - row_mean(e) - norm * row_mean(e * norm))
        acc[rows, :] = first
        low[rows, :] = first.astype(BF16)
        sum_attn[...] += jnp.sum(g, axis=0, keepdims=True)
        sum_out[...] += jnp.sum(first, axis=0, keepdims=True)

    @pl.loop(0, width // tile)
    def _(i):
        cols = pl.ds(pl.multiple_of(i * tile, tile), tile)
        gctx[:, cols] = dot(low[...], wo[:, cols]).astype(BF16)

    @pl.loop(0, pairs)
    def _(i):
        cols = pl.ds(pl.multiple_of(i * 128, 128), 128)
        q2 = qs[:, cols]
        k2t = ks[:, cols].T
        v2 = vs[:, cols]
        g2 = gctx[:, cols]
        dq, dk, dv = [], [], []
        for hh in range(2):
            p = probs[2 * i + hh]
            pf = p.astype(F32)
            dpt = dot(half_of(v2, hh), g2, NT)
            ds = (pf * (dpt - jnp.sum(pf * dpt, axis=0, keepdims=True))).astype(BF16)
            dk.append(dot(ds, q2))
            dv.append(dot(p, g2))
            dq.append(dot(k2t[hh * HEAD_DIM:(hh + 1) * HEAD_DIM], ds))
        dq2 = jnp.concatenate(dq, axis=0).T.astype(BF16).astype(F32) * scale
        dv2 = jnp.where(lane < HEAD_DIM, dv[0], dv[1]).astype(BF16)
        qs[:, cols] = dq2.astype(BF16)
        ks[:, cols] = jnp.where(lane < HEAD_DIM, dk[0], dk[1]).astype(BF16)
        vs[:, cols] = dv2
        sum_q[:, cols] = jnp.sum(dq2, axis=0, keepdims=True)
        sum_v[:, cols] = jnp.sum(dv2.astype(F32), axis=0, keepdims=True)

    side = seq // 2
    per = mp // 2
    mine = z // per
    for turn in range(2):
        block = 1 - mine if turn == 0 else mine
        rows = pl.ds(pl.multiple_of(block * side, side), side)

        @pl.loop(0, width // tile)
        def _(i):
            cols = pl.ds(pl.multiple_of(i * tile, tile), tile)
            x = acc[rows, cols]
            x += dot(qs[rows, :], wq[0, cols, :], NT)
            x += dot(ks[rows, :], wq[1, cols, :], NT)
            x += dot(vs[rows, :], wq[2, cols, :], NT)
            xh[rows, cols] = x.astype(BF16)

        for q in range(per):
            there = block * per + (z + q + turn) % per
            if turn == 0 or q < per - 1:
                push_out(xh, grad, 3, there)
    keep_grad = pltpu.make_async_copy(tokens(xh, z), grad.at[z], local_sem.at[7])
    keep_grad.start()

    keep_out.wait()
    keep_grad.wait()
    for which, src in ((0, tokens(xh, z)), (1, tokens(xh, z)), (2, tokens(xh, z)), (3, tokens(xh, z))):
        sends_wait(src, which)
    for which, ref in ((2, out), (3, grad)):
        for hop in range(1, mp):
            there = (z + hop) % mp
            pltpu.make_async_copy(ref.at[there], ref.at[there], row_recv.at[which, there]).wait()
    for b in range(4):
        ref = wholes[b]
        cols = (cq if b < 2 else cu) * mp
        ways = (
            (rb * (2 * half - 1), cols // 2),
            (rb * (2 * half - 1), cols // 2),
            (width // 2, cols),
            (rb, cols - cols // mp),
        )
        for way, (r, c) in enumerate(ways):
            part = ref.at[:, pl.ds(0, r), pl.ds(0, c)] if b == 0 else ref.at[pl.ds(0, r), pl.ds(0, c)]
            pltpu.make_async_copy(part, part, send_sem.at[b, way]).wait()


def on_device(
    hidden_in, lengths, separators, seg_table, query_key_value_weight, output_weight, up_weight, down_weight,
    bias_q, bias_v, bias_out, expand_bias, bias_down, gain_attn, shift_attn, gain_ffn, shift_ffn, cotangent,
):
    dp, mp = lax.axis_size("dp"), lax.axis_size("mp")
    here, tok, width = hidden_in.shape
    assert here == mp
    seq = tok * mp
    units = up_weight.shape[1] * mp
    heads = width // HEAD_DIM
    vmem = pl.BlockSpec(memory_space=pltpu.VMEM)
    smem = pl.BlockSpec(memory_space=pltpu.SMEM)
    anys = pl.BlockSpec(memory_space=pl.ANY)
    rows = [seg_table] + [
        v.reshape(1, -1)
        for v in (bias_q, bias_v, bias_out, expand_bias, bias_down, gain_attn, shift_attn, gain_ffn, shift_ffn)
    ]
    vec = jax.ShapeDtypeStruct((1, width), F32)
    moved = jax.ShapeDtypeStruct(hidden_in.shape, BF16)
    ring = dp // 2
    sem = pltpu.SemaphoreType.DMA
    results = pl.pallas_call(
        functools.partial(step_kernel, (dp, mp, seq, width, units)),
        name="step",
        out_shape=(moved, moved, vec, vec, vec, jax.ShapeDtypeStruct((1, units), F32), vec, vec, vec),
        in_specs=[smem, smem] + [vmem] * 10 + [anys] * 6,
        out_specs=(anys, anys) + (vmem,) * 7,
        scratch_shapes=[
            pltpu.VMEM((3, width, width), BF16),
            pltpu.VMEM((width, width), BF16),
            pltpu.VMEM((width, units), BF16),
            pltpu.VMEM((width, units), BF16),
            *[pltpu.VMEM((seq, width), BF16)] * 7,
            pltpu.VMEM((heads, seq, seq), BF16),
            pltpu.VMEM((seq, width), F32),
            pltpu.VMEM((seq, 128), F32),
            pltpu.VMEM((seq, width), F32),
            pltpu.VMEM((seq, units), BF16),
            pltpu.VMEM((seq, units), BF16),
            pltpu.VMEM((seq, width), BF16),
            sem((8,)),
            sem((6, mp, ring)),
            sem((6, mp)),
            sem((4, 4)),
            sem((4, mp)),
            sem((4, mp)),
        ],
        compiler_params=pltpu.CompilerParams(collective_id=0, has_side_effects=True, vmem_limit_bytes=67043328),
    )(
        lengths, separators, *rows, hidden_in, cotangent, jnp.swapaxes(query_key_value_weight, 0, 1),
        output_weight, up_weight, down_weight,
    )
    factor = 1.0 / (here * seq * dp)
    sums = lax.psum(tuple(s.reshape(-1) for s in results[2:]), ("dp", "mp"))
    return results[:2] + tuple(s * factor for s in sums)


def solution(mesh):
    rows = P("dp", "mp", None)
    frozen = P("dp", "mp")
    placed = (rows, P("dp"), P("dp"), P(), P("dp", None, "mp"), frozen, frozen, frozen) + (P(),) * 9 + (rows,)
    return jax.shard_map(on_device, mesh=mesh, in_specs=placed, out_specs=(rows, rows) + (P(),) * 7, check_vma=False)
```

```python
import functools
import math

import jax
import jax.numpy as jnp
from jax import lax
from jax.experimental import pallas as pl
from jax.experimental.pallas import tpu as pltpu
from jax.sharding import PartitionSpec as P

HEAD_DIM = 64
EPS = 1e-12
F32 = jnp.float32
BF16 = jnp.bfloat16
MESH = pl.DeviceIdType.MESH
ROWS = 64
LAG = 0
NN = ((1,), (0,))
NT = ((1,), (1,))


def dot(a, b, dims=NN):
    return lax.dot_general(a, b, (dims, ((), ())), preferred_element_type=F32)


def snake(pos):
    high = pos // 2
    return 2 * high + (pos % 2 + high) % 2


def row_mean(x):
    return jnp.sum(x, axis=-1, keepdims=True) * (1.0 / x.shape[-1])


def step_kernel(
    shape, lens, seps, seg, bias_q, bias_v, bias_out, expand_bias, bias_down, gain_attn, shift_attn, gain_ffn,
    shift_ffn, hid, cot, wq_in, wo_in, wu_in, wd_in,
    out, grad, sums,
    wq, wo, wu, wd, xh, ct, outb, low, qs, ks, vs, probs, normal, inverse, acc, act, slope, gctx,
    early, late, inbox, local_sem, ici_sem, sib_sem, send_sem, row_recv, row_send, sum_recv, sum_send,
):
    dp, mp, seq, width, units = shape
    ring, half = dp // 2, dp // 4
    rb = width // dp
    cq = width // mp
    cu = units // mp
    hu = cu // 2
    tok = seq // mp
    heads = width // HEAD_DIM
    scale = 1.0 / math.sqrt(HEAD_DIM)
    d = lax.axis_index("dp")
    z = lax.axis_index("mp")
    core = d % 2
    pos = snake(d // 2)
    right = (2 * snake((pos + 1) % ring) + core, z)
    left = (2 * snake((pos + ring - 1) % ring) + core, z)
    sibling = (d + 1 - 2 * core, z)
    wholes = (wq, wo, wu, wd)
    shards = (wq_in, wo_in, wu_in, wd_in)

    def region(b, j, k, origin):
        zz = (z + mp - k) % mp
        rows = pl.ds(pl.multiple_of((2 * snake(origin) + core) * rb, rb), rb)
        if b == 0:
            return wq.at[:, rows, pl.ds(pl.multiple_of(zz * cq, 128), cq)]
        if b == 1:
            return wo.at[rows, pl.ds(pl.multiple_of(zz * cq, 128), cq)]
        return wholes[b].at[rows, pl.ds(pl.multiple_of(zz * cu + j * hu, 128), hu)]

    def own_shard(b, j):
        if b < 2:
            return shards[b]
        return shards[b].at[:, pl.ds(pl.multiple_of(j * hu, 128), hu)]

    def piece(b, j):
        return (0, 1, 2, 4)[b] + j

    def send(src, b, j, k, origin, way, target):
        zz = (z + mp - k) % mp
        dst = region(b, j, k, origin)
        recv = sib_sem.at[piece(b, j), zz] if way == 2 else ici_sem.at[piece(b, j), zz, origin]
        pltpu.make_async_remote_copy(
            src_ref=src, dst_ref=dst, send_sem=send_sem.at[b, way], recv_sem=recv, device_id=target, device_id_type=MESH
        ).start()

    def arrived(b, j, k, origin):
        zz = (z + mp - k) % mp
        ref = region(b, j, k, origin)
        pltpu.make_async_copy(ref, ref, ici_sem.at[piece(b, j), zz, origin]).wait()
        return ref

    def spread(src, b, j, k):
        send(src, b, j, k, pos, 0, right)
        send(src, b, j, k, pos, 1, left)
        send(src, b, j, k, pos, 2, sibling)

    def start_own(b, j):
        for hop in range(1, mp):
            there = (z + hop) % mp
            send_z(b, j, there)
        spread(own_shard(b, j), b, j, 0)

    def send_z(b, j, there):
        pltpu.make_async_remote_copy(
            src_ref=own_shard(b, j), dst_ref=region(b, j, 0, pos), send_sem=send_sem.at[b, 3],
            recv_sem=ici_sem.at[piece(b, j), z, pos], device_id=(d, there), device_id_type=MESH,
        ).start()

    def serve_column(b, j, k):
        spread(arrived(b, j, k, pos), b, j, k)

    def pick(cond, fn):
        if isinstance(cond, bool):
            if cond:
                fn()
        else:
            pl.when(cond)(fn)

    def serve_ring(b, j, k, dist):
        even, odd = k % 2 == 0, k % 2 == 1

        def from_left():
            origin = (pos + ring - dist) % ring
            ref = arrived(b, j, k, origin)
            if dist + 1 < half:
                send(ref, b, j, k, origin, 0, right)
            elif dist + 1 == half:
                pick(even, lambda: send(ref, b, j, k, origin, 0, right))
            send(ref, b, j, k, origin, 2, sibling)

        def from_right():
            origin = (pos + dist) % ring
            ref = arrived(b, j, k, origin)
            if dist + 1 < half:
                send(ref, b, j, k, origin, 1, left)
            elif dist + 1 == half:
                pick(odd, lambda: send(ref, b, j, k, origin, 1, left))
            send(ref, b, j, k, origin, 2, sibling)

        if dist < half:
            from_left()
            from_right()
        else:
            pick(even, from_left)
            pick(odd, from_right)

    total_items = 6 * mp
    bounds = (0, mp, 2 * mp, 4 * mp, total_items)
    lag = half + LAG

    def with_item(u, low_u, high_u, fn):
        if isinstance(u, int):
            if 0 <= u < total_items:
                b = sum(u >= x for x in bounds[1:4])
                fn(b, (u - bounds[b]) // mp, (u - bounds[b]) % mp)
            return
        for b in range(4):
            if low_u < bounds[b + 1] and high_u >= bounds[b]:
                inside = True
                if low_u < bounds[b]:
                    inside = u >= bounds[b]
                if high_u >= bounds[b + 1]:
                    inside = (u < bounds[b + 1]) if inside is True else jnp.logical_and(inside, u < bounds[b + 1])
                pick(inside, lambda b=b: fn(b, (u - bounds[b]) // mp, (u - bounds[b]) % mp))

    def tick(t, low_t=0, high_t=0):
        with_item(t, low_t, high_t, lambda b, j, k: pick(k > 0, lambda: serve_column(b, j, k)))
        for dist in range(1, half + 1):
            back = dist + LAG
            with_item(t - back, low_t - back, high_t - back, lambda b, j, k: serve_ring(b, j, k, dist))

    def sibling_done(b, j, k):
        zz = (z + mp - k) % mp
        if b == 0:
            ref = wq.at[:, pl.ds(0, width // 2), pl.ds(0, cq)]
        elif b == 1:
            ref = wo.at[pl.ds(0, width // 2), pl.ds(0, cq)]
        else:
            ref = wholes[b].at[pl.ds(0, width // 2), pl.ds(0, hu)]
        pltpu.make_async_copy(ref, ref, sib_sem.at[piece(b, j), zz]).wait()

    def tokens(ref, block):
        return ref.at[pl.ds(pl.multiple_of(block * tok, tok), tok), :]

    def own_local(b):
        zz = z
        rows = pl.ds(pl.multiple_of(d * rb, rb), rb)
        if b == 0:
            dst = wq.at[:, rows, pl.ds(pl.multiple_of(zz * cq, 128), cq)]
        elif b == 1:
            dst = wo.at[rows, pl.ds(pl.multiple_of(zz * cq, 128), cq)]
        else:
            dst = wholes[b].at[rows, pl.ds(pl.multiple_of(zz * cu, 128), cu)]
        return pltpu.make_async_copy(shards[b], dst, local_sem.at[b])

    barrier = pltpu.get_barrier_semaphore()
    def flip(index, bit):
        return index + bit - 2 * bit * ((index // bit) % 2)

    peers = [(d, flip(z, 1 << s)) for s in range(mp.bit_length() - 1)]
    peers += [(flip(d, 1 << s), z) for s in range(1, dp.bit_length() - 1)] + [sibling]
    partners = [sibling, right, left] + [(d, (z + hop) % mp) for hop in range(1, mp)] + peers
    for target in partners:
        pl.semaphore_signal(barrier, inc=1, device_id=target, device_id_type=MESH)
    for b in range(4):
        own_local(b).start()
    own_hid = pltpu.make_async_copy(hid.at[z], tokens(xh, z), local_sem.at[4])
    own_cot = pltpu.make_async_copy(cot.at[z], tokens(ct, z), local_sem.at[5])
    own_hid.start()
    own_cot.start()
    pl.semaphore_wait(barrier, len(partners))

    def exchange_in(src, dst, which):
        for hop in range(1, mp):
            there = (z + hop) % mp
            pltpu.make_async_remote_copy(
                src_ref=src.at[there], dst_ref=tokens(dst, z), send_sem=row_send.at[which, there],
                recv_sem=row_recv.at[which, z], device_id=(d, there), device_id_type=MESH,
            ).start()

    def exchange_wait(src, dst, which):
        for hop in range(1, mp):
            there = (z + hop) % mp
            pltpu.make_async_copy(tokens(dst, there), tokens(dst, there), row_recv.at[which, there]).wait()

    def sends_wait(ref, which):
        for hop in range(1, mp):
            there = (z + hop) % mp
            pltpu.make_async_copy(ref, ref, row_send.at[which, there]).wait()

    start_own(0, 0)
    exchange_in(hid, xh, 0)
    start_own(1, 0)
    for b in (2, 3):
        for j in range(2):
            start_own(b, j)
    exchange_in(cot, ct, 1)

    ready = lag + 1
    for t in range(mp + ready):
        tick(t)
    own_hid.wait()
    exchange_wait(hid, xh, 0)
    length = lens[z]
    separator = seps[z]
    seg0 = seg[0:1, :]
    seg_step = seg[1:2, :] - seg[0:1, :]

    def embed(rows, first):
        at = lax.broadcasted_iota(jnp.int32, (ROWS, 1), 0) + first
        flag = jnp.where(at > separator, 1.0, 0.0).astype(F32)
        return xh[rows, :].astype(F32) + seg0 + flag * seg_step

    @pl.loop(0, seq // ROWS)
    def _(i):
        first = pl.multiple_of(i * ROWS, ROWS)
        rows = pl.ds(first, ROWS)
        low[rows, :] = embed(rows, first).astype(BF16)

    own_local(0).wait()
    for k in range(mp):
        sibling_done(0, 0, k)

    tile = 256

    @pl.loop(0, width // tile)
    def _(i):
        cols = pl.ds(pl.multiple_of(i * tile, tile), tile)
        qs[:, cols] = ((dot(low[...], wq[0, :, cols]) + bias_q[:, cols]) * scale).astype(BF16)
        ks[:, cols] = dot(low[...], wq[1, :, cols]).astype(BF16)
        vs[:, cols] = (dot(low[...], wq[2, :, cols]) + bias_v[:, cols]).astype(BF16)

    pairs = heads // 2
    lane = lax.broadcasted_iota(jnp.int32, (seq, 2 * HEAD_DIM), 1)

    def half_of(x, hh):
        keep = lane < HEAD_DIM if hh == 0 else lane >= HEAD_DIM
        return jnp.where(keep, x, jnp.zeros_like(x))

    items = 2 * mp

    @pl.loop(0, pairs)
    def _(i):
        @pl.when(i % (pairs // mp) == 0)
        def _():
            tick(mp + ready + i // (pairs // mp), mp + ready, 2 * mp + ready - 1)

        cols = pl.ds(pl.multiple_of(i * 128, 128), 128)
        q2 = qs[:, cols]
        k2 = ks[:, cols]
        v2t = vs[:, cols].T
        ctxs = []
        for hh in range(2):
            st = dot(half_of(k2, hh), q2, NT)
            valid = lax.broadcasted_iota(jnp.int32, st.shape, 0) < length
            st = jnp.where(valid, st, -1e30)
            e = jnp.exp(st - jnp.max(st, axis=0, keepdims=True))
            p = (e * (1.0 / jnp.sum(e, axis=0, keepdims=True))).astype(BF16)
            probs[2 * i + hh] = p
            ctxs.append(dot(v2t[hh * HEAD_DIM:(hh + 1) * HEAD_DIM], p))
        low[:, cols] = jnp.concatenate(ctxs, axis=0).T.astype(BF16)

    own_local(1).wait()
    for k in range(mp):
        sibling_done(1, 0, k)

    @pl.loop(0, width // tile)
    def _(i):
        cols = pl.ds(pl.multiple_of(i * tile, tile), tile)
        acc[:, cols] = dot(low[...], wo[cols, :], NT)

    @pl.loop(0, seq // ROWS)
    def _(i):
        first = pl.multiple_of(i * ROWS, ROWS)
        rows = pl.ds(first, ROWS)
        x = embed(rows, first) + acc[rows, :] + bias_out[...]
        center = x - row_mean(x)
        inv = lax.rsqrt(row_mean(center * center) + EPS)
        norm = center * inv
        normal[rows, :] = norm
        inverse[rows, :] = jnp.broadcast_to(inv, (ROWS, 128))
        low[rows, :] = (norm * gain_attn[...] + shift_attn[...]).astype(BF16)
        acc[rows, :] = jnp.zeros((ROWS, width), F32)

    own_local(2).wait()

    def slab(i):
        zz = (z + mp - i % mp) % mp
        return pl.multiple_of(zz * cu + (i // mp) * hu, 128)

    @pl.loop(0, items)
    def _(i):
        tick(2 * mp + ready + i, 2 * mp + ready, 4 * mp + ready - 1)
        sibling_done(2, i // mp, i % mp)
        base = slab(i)

        @pl.loop(0, hu // tile)
        def _(n):
            cols = pl.ds(pl.multiple_of(base + n * tile, 128), tile)
            inner = dot(low[...], wu[:, cols]) + expand_bias[:, cols]
            cdf = 0.5 * (1.0 + lax.erf(inner * math.sqrt(0.5)))
            act[:, cols] = (inner * cdf).astype(BF16)
            bell = jnp.exp(-0.5 * inner * inner) * (1.0 / math.sqrt(2.0 * math.pi))
            slope[:, cols] = (cdf + inner * bell).astype(BF16)

    own_local(3).wait()

    @pl.loop(0, items)
    def _(i):
        tick(4 * mp + ready + i, 4 * mp + ready, 6 * mp + ready - 1)
        sibling_done(3, i // mp, i % mp)
        cols = pl.ds(slab(i), hu)

        @pl.loop(0, width // 512)
        def _(n):
            rows = pl.ds(pl.multiple_of(n * 512, 512), 512)
            acc[:, rows] += dot(act[:, cols], wd[rows, cols], NT)

    own_cot.wait()
    exchange_wait(cot, ct, 1)
    early[0] = jnp.zeros(early.shape[1:], F32)
    late[0] = jnp.zeros(late.shape[1:], F32)

    @pl.loop(0, seq // ROWS)
    def _(i):
        rows = pl.ds(pl.multiple_of(i * ROWS, ROWS), ROWS)
        x = normal[rows, :] * gain_attn[...] + shift_attn[...] + acc[rows, :] + bias_down[...]
        center = x - row_mean(x)
        inv = lax.rsqrt(row_mean(center * center) + EPS)
        norm = center * inv
        outb[rows, :] = (norm * gain_ffn[...] + shift_ffn[...]).astype(BF16)
        dy = ct[rows, :].astype(F32)
        e = dy * gain_ffn[...]
        g = inv * (e - row_mean(e) - norm * row_mean(e * norm))
        acc[rows, :] = g
        low[rows, :] = g.astype(BF16)
        early[0, 0:1, :] += jnp.sum(dy, axis=0, keepdims=True)
        early[0, 1:2, :] += jnp.sum(g, axis=0, keepdims=True)

    def push_out(buf, dst, which, there):
        pltpu.make_async_remote_copy(
            src_ref=tokens(buf, there), dst_ref=dst.at[z], send_sem=row_send.at[which, there],
            recv_sem=row_recv.at[which, z], device_id=(d, there), device_id_type=MESH,
        ).start()

    for hop in range(1, mp):
        push_out(outb, out, 2, (z + hop) % mp)
    keep_out = pltpu.make_async_copy(tokens(outb, z), out.at[z], local_sem.at[6])
    keep_out.start()

    for part in range(units // width):

        @pl.loop(0, width // tile)
        def _(i):
            here = pl.ds(pl.multiple_of(i * tile, tile), tile)
            cols = pl.ds(pl.multiple_of(part * width + i * tile, tile), tile)
            g = (dot(low[...], wd[:, cols]) * slope[:, cols].astype(F32)).astype(BF16)
            act[:, cols] = g
            early[0, 4 + part:5 + part, here] = jnp.sum(g.astype(F32), axis=0, keepdims=True)

    @pl.loop(0, width // tile)
    def _(i):
        cols = pl.ds(pl.multiple_of(i * tile, tile), tile)
        acc[:, cols] += dot(act[...], wu[cols, :], NT)

    @pl.loop(0, seq // ROWS)
    def _(i):
        rows = pl.ds(pl.multiple_of(i * ROWS, ROWS), ROWS)
        g = acc[rows, :]
        norm = normal[rows, :]
        e = g * gain_attn[...]
        first = inverse[rows, 0:1] * (e - row_mean(e) - norm * row_mean(e * norm))
        acc[rows, :] = first
        low[rows, :] = first.astype(BF16)
        early[0, 2:3, :] += jnp.sum(g, axis=0, keepdims=True)
        early[0, 3:4, :] += jnp.sum(first, axis=0, keepdims=True)

    @pl.loop(0, width // tile)
    def _(i):
        cols = pl.ds(pl.multiple_of(i * tile, tile), tile)
        gctx[:, cols] = dot(low[...], wo[:, cols]).astype(BF16)

    def sum_send_step(buf, which, s):
        pltpu.make_async_remote_copy(
            src_ref=buf.at[s], dst_ref=inbox.at[which, s], send_sem=sum_send.at[which, s],
            recv_sem=sum_recv.at[which, s], device_id=peers[s], device_id_type=MESH,
        ).start()

    def sum_take_step(buf, which, s):
        pltpu.make_async_copy(inbox.at[which, s], inbox.at[which, s], sum_recv.at[which, s]).wait()
        buf[s + 1] = buf[s] + inbox[which, s]

    steps = len(peers)
    sum_send_step(early, 0, 0)

    @pl.loop(0, pairs)
    def _(i):
        for s in range(steps):

            @pl.when(i == min(s + 1, pairs - 1))
            def _(s=s):
                sum_take_step(early, 0, s)
                if s + 1 < steps:
                    sum_send_step(early, 0, s + 1)

        cols = pl.ds(pl.multiple_of(i * 128, 128), 128)
        q2 = qs[:, cols]
        k2t = ks[:, cols].T
        v2 = vs[:, cols]
        g2 = gctx[:, cols]
        dq, dk, dv = [], [], []
        for hh in range(2):
            p = probs[2 * i + hh]
            pf = p.astype(F32)
            dpt = dot(half_of(v2, hh), g2, NT)
            ds = (pf * (dpt - jnp.sum(pf * dpt, axis=0, keepdims=True))).astype(BF16)
            dk.append(dot(ds, q2))
            dv.append(dot(p, g2))
            dq.append(dot(k2t[hh * HEAD_DIM:(hh + 1) * HEAD_DIM], ds))
        dq2 = jnp.concatenate(dq, axis=0).T.astype(BF16).astype(F32) * scale
        dv2 = jnp.where(lane < HEAD_DIM, dv[0], dv[1]).astype(BF16)
        qs[:, cols] = dq2.astype(BF16)
        ks[:, cols] = jnp.where(lane < HEAD_DIM, dk[0], dk[1]).astype(BF16)
        vs[:, cols] = dv2
        late[0, 0:1, cols] = jnp.sum(dq2, axis=0, keepdims=True)
        late[0, 1:2, cols] = jnp.sum(dv2.astype(F32), axis=0, keepdims=True)

    sum_send_step(late, 1, 0)
    side = seq // 2
    per = mp // 2
    mine = z // per
    for turn in range(2):
        block = 1 - mine if turn == 0 else mine
        rows = pl.ds(pl.multiple_of(block * side, side), side)

        @pl.loop(0, width // tile)
        def _(i):
            for u in range(2):
                s = 2 * turn + u

                @pl.when(i == 2 * u + 1)
                def _(s=s):
                    sum_take_step(late, 1, s)
                    sum_send_step(late, 1, s + 1)

            cols = pl.ds(pl.multiple_of(i * tile, tile), tile)
            x = acc[rows, cols]
            x += dot(qs[rows, :], wq[0, cols, :], NT)
            x += dot(ks[rows, :], wq[1, cols, :], NT)
            x += dot(vs[rows, :], wq[2, cols, :], NT)
            xh[rows, cols] = x.astype(BF16)

        for q in range(per):
            there = block * per + (z + q + turn) % per
            if turn == 0 or q < per - 1:
                push_out(xh, grad, 3, there)
    keep_grad = pltpu.make_async_copy(tokens(xh, z), grad.at[z], local_sem.at[7])
    keep_grad.start()

    for s in range(4, steps):
        sum_take_step(late, 1, s)
        if s + 1 < steps:
            sum_send_step(late, 1, s + 1)
    sums[0] = early[steps]
    sums[1] = late[steps]
    for which, buf in ((0, early), (1, late)):
        for s in range(steps):
            pltpu.make_async_copy(buf.at[s], buf.at[s], sum_send.at[which, s]).wait()

    keep_out.wait()
    keep_grad.wait()
    for which, src in ((0, tokens(xh, z)), (1, tokens(xh, z)), (2, tokens(xh, z)), (3, tokens(xh, z))):
        sends_wait(src, which)
    for which, ref in ((2, out), (3, grad)):
        for hop in range(1, mp):
            there = (z + hop) % mp
            pltpu.make_async_copy(ref.at[there], ref.at[there], row_recv.at[which, there]).wait()
    for b in range(4):
        ref = wholes[b]
        cols = (cq if b < 2 else cu) * mp
        ways = (
            (rb * (2 * half - 1), cols // 2),
            (rb * (2 * half - 1), cols // 2),
            (width // 2, cols),
            (rb, cols - cols // mp),
        )
        for way, (r, c) in enumerate(ways):
            part = ref.at[:, pl.ds(0, r), pl.ds(0, c)] if b == 0 else ref.at[pl.ds(0, r), pl.ds(0, c)]
            pltpu.make_async_copy(part, part, send_sem.at[b, way]).wait()


def on_device(
    hidden_in, lengths, separators, seg_table, query_key_value_weight, output_weight, up_weight, down_weight,
    bias_q, bias_v, bias_out, expand_bias, bias_down, gain_attn, shift_attn, gain_ffn, shift_ffn, cotangent,
):
    dp, mp = lax.axis_size("dp"), lax.axis_size("mp")
    here, tok, width = hidden_in.shape
    assert here == mp
    seq = tok * mp
    units = up_weight.shape[1] * mp
    heads = width // HEAD_DIM
    vmem = pl.BlockSpec(memory_space=pltpu.VMEM)
    smem = pl.BlockSpec(memory_space=pltpu.SMEM)
    anys = pl.BlockSpec(memory_space=pl.ANY)
    rows = [seg_table] + [
        v.reshape(1, -1)
        for v in (bias_q, bias_v, bias_out, expand_bias, bias_down, gain_attn, shift_attn, gain_ffn, shift_ffn)
    ]
    steps = dp.bit_length() + mp.bit_length() - 2
    summed = (4 + units // width, width)
    moved = jax.ShapeDtypeStruct(hidden_in.shape, BF16)
    ring = dp // 2
    sem = pltpu.SemaphoreType.DMA
    results = pl.pallas_call(
        functools.partial(step_kernel, (dp, mp, seq, width, units)),
        name="step",
        out_shape=(moved, moved, jax.ShapeDtypeStruct((2,) + summed, F32)),
        in_specs=[smem, smem] + [vmem] * 10 + [anys] * 6,
        out_specs=(anys, anys, vmem),
        scratch_shapes=[
            pltpu.VMEM((3, width, width), BF16),
            pltpu.VMEM((width, width), BF16),
            pltpu.VMEM((width, units), BF16),
            pltpu.VMEM((width, units), BF16),
            *[pltpu.VMEM((seq, width), BF16)] * 7,
            pltpu.VMEM((heads, seq, seq), BF16),
            pltpu.VMEM((seq, width), F32),
            pltpu.VMEM((seq, 128), F32),
            pltpu.VMEM((seq, width), F32),
            pltpu.VMEM((seq, units), BF16),
            pltpu.VMEM((seq, units), BF16),
            pltpu.VMEM((seq, width), BF16),
            pltpu.VMEM((steps + 1,) + summed, F32),
            pltpu.VMEM((steps + 1,) + summed, F32),
            pltpu.VMEM((2, steps) + summed, F32),
            sem((8,)),
            sem((6, mp, ring)),
            sem((6, mp)),
            sem((4, 4)),
            sem((4, mp)),
            sem((4, mp)),
            sem((2, steps)),
            sem((2, steps)),
        ],
        compiler_params=pltpu.CompilerParams(collective_id=0, has_side_effects=True, vmem_limit_bytes=67043328),
    )(
        lengths, separators, *rows, hidden_in, cotangent, jnp.swapaxes(query_key_value_weight, 0, 1),
        output_weight, up_weight, down_weight,
    )
    sums = results[2] * (1.0 / (here * seq * dp))
    first, last = sums[0], sums[1]
    return results[:2] + (last[0], last[1], first[3], first[4:].reshape(-1), first[1], first[2], first[0])


def solution(mesh):
    rows = P("dp", "mp", None)
    frozen = P("dp", "mp")
    placed = (rows, P("dp"), P("dp"), P(), P("dp", None, "mp"), frozen, frozen, frozen) + (P(),) * 9 + (rows,)
    return jax.shard_map(on_device, mesh=mesh, in_specs=placed, out_specs=(rows, rows) + (P(),) * 7, check_vma=False)
```

```python
import functools
import math

import jax
import jax.numpy as jnp
from jax import lax
from jax.experimental import pallas as pl
from jax.experimental.pallas import tpu as pltpu
from jax.sharding import PartitionSpec as P

HEAD_DIM = 64
EPS = 1e-12
F32 = jnp.float32
BF16 = jnp.bfloat16
MESH = pl.DeviceIdType.MESH
ROWS = 64
LAG = 0
PLAN = {0: (1,), 3: (2,), 6: (3,), 9: (4,), 12: (5,)}
HID_AT = {1: (1,2,3)}
COT_AT = {16: (1,2,3)}
QKV_TICKS = 2
ATTN_TICKS = 4
UP_TICKS = 6
NN = ((1,), (0,))
NT = ((1,), (1,))


def dot(a, b, dims=NN):
    return lax.dot_general(a, b, (dims, ((), ())), preferred_element_type=F32)


def snake(pos):
    high = pos // 2
    return 2 * high + (pos % 2 + high) % 2


def row_mean(x):
    return jnp.sum(x, axis=-1, keepdims=True) * (1.0 / x.shape[-1])


def step_kernel(
    shape, lens, seps, seg, bias_q, bias_v, bias_out, expand_bias, bias_down, gain_attn, shift_attn, gain_ffn,
    shift_ffn, hid, cot, wq_in, wo_in, wu_in, wd_in,
    out, grad, sums,
    wq, wo, wu, wd, xh, ct, outb, low, qs, ks, vs, probs, normal, inverse, acc, act, slope, gctx,
    early, late, inbox, local_sem, ici_sem, sib_sem, send_sem, row_recv, row_send, sum_recv, sum_send,
):
    dp, mp, seq, width, units = shape
    ring, half = dp // 2, dp // 4
    rb = width // dp
    cq = width // mp
    cu = units // mp
    hu = cu // 2
    tok = seq // mp
    heads = width // HEAD_DIM
    scale = 1.0 / math.sqrt(HEAD_DIM)
    d = lax.axis_index("dp")
    z = lax.axis_index("mp")
    core = d % 2
    pos = snake(d // 2)
    right = (2 * snake((pos + 1) % ring) + core, z)
    left = (2 * snake((pos + ring - 1) % ring) + core, z)
    sibling = (d + 1 - 2 * core, z)
    wholes = (wq, wo, wu, wd)
    shards = (wq_in, wo_in, wu_in, wd_in)

    def region(b, j, k, origin):
        zz = (z + mp - k) % mp
        rows = pl.ds(pl.multiple_of((2 * snake(origin) + core) * rb, rb), rb)
        if b == 0:
            return wq.at[:, rows, pl.ds(pl.multiple_of(zz * cq, 128), cq)]
        if b == 1:
            return wo.at[rows, pl.ds(pl.multiple_of(zz * cq, 128), cq)]
        return wholes[b].at[rows, pl.ds(pl.multiple_of(zz * cu + j * hu, 128), hu)]

    def own_shard(b, j):
        if b < 2:
            return shards[b]
        return shards[b].at[:, pl.ds(pl.multiple_of(j * hu, 128), hu)]

    def piece(b, j):
        return (0, 1, 2, 4)[b] + j

    def send(src, b, j, k, origin, way, target, part=()):
        zz = (z + mp - k) % mp
        dst = region(b, j, k, origin).at[part] if part else region(b, j, k, origin)
        recv = sib_sem.at[piece(b, j), zz] if way == 2 else ici_sem.at[piece(b, j), zz, origin]
        pltpu.make_async_remote_copy(
            src_ref=src, dst_ref=dst, send_sem=send_sem.at[b, way], recv_sem=recv, device_id=target, device_id_type=MESH
        ).start()

    def arrived(b, j, k, origin):
        zz = (z + mp - k) % mp
        ref = region(b, j, k, origin)
        pltpu.make_async_copy(ref, ref, ici_sem.at[piece(b, j), zz, origin]).wait()
        return ref

    def spread(src, b, j, k):
        send(src, b, j, k, pos, 0, right)
        send(src, b, j, k, pos, 1, left)
        send(src, b, j, k, pos, 2, sibling)

    def start_own(b, j):
        spread(own_shard(b, j), b, j, 0)

    def send_z(b, j, there):
        pltpu.make_async_remote_copy(
            src_ref=own_shard(b, j), dst_ref=region(b, j, 0, pos), send_sem=send_sem.at[b, 3],
            recv_sem=ici_sem.at[piece(b, j), z, pos], device_id=(d, there), device_id_type=MESH,
        ).start()

    def serve_column(b, j, k):
        spread(arrived(b, j, k, pos), b, j, k)

    def pick(cond, fn):
        if isinstance(cond, bool):
            if cond:
                fn()
        else:
            pl.when(cond)(fn)

    def relay(ref, b, j, k, origin, way, target):
        part = (slice(None),) * (b == 0) + (pl.ds(way * (rb // 2), rb // 2),)
        send(ref.at[part], b, j, k, origin, way, target, part)

    def serve_ring(b, j, k, dist):
        if dist == half:
            origin = (pos + half) % ring
            send(arrived(b, j, k, origin), b, j, k, origin, 2, sibling)
            return
        pass_on = relay if dist + 1 == half else send
        for way, origin, target in ((0, (pos + ring - dist) % ring, right), (1, (pos + dist) % ring, left)):
            ref = arrived(b, j, k, origin)
            pass_on(ref, b, j, k, origin, way, target)
            send(ref, b, j, k, origin, 2, sibling)

    pieces = ((0, 0), (1, 0), (2, 0), (2, 1), (3, 0), (3, 1))
    order = [(b, j, 0) for b, j in pieces] + [(b, j, k) for b, j in pieces for k in range(1, mp)]
    lag = half + LAG
    served = [0]

    def with_item(t, fn):
        if 0 <= t < len(order):
            fn(*order[t])

    def tick(t):
        with_item(t, lambda b, j, k: k > 0 and serve_column(b, j, k))
        for dist in range(1, half + 1):
            with_item(t - dist - LAG, lambda b, j, k: serve_ring(b, j, k, dist))

    def column_out(p):
        for hop in range(1, mp):
            send_z(*pieces[p], (z + hop) % mp)

    def serve_to(count):
        for t in range(served[0], count):
            for p in PLAN.get(t, ()):
                column_out(p)
            for hop in HID_AT.get(t, ()):
                exchange_in(hid, xh, 0, hop)
            for hop in COT_AT.get(t, ()):
                exchange_in(cot, ct, 1, hop)
            tick(t)
        served[0] = max(served[0], count)

    def whole_at(b, j, k):
        return order.index((b, j, k)) + lag + 1

    def serve_within(i, slots, until):
        first = served[0]
        for slot in range(slots):
            upto = min(until(slot), len(order) + lag)
            if upto > served[0]:
                pl.when(i == slot)(functools.partial(serve_to, upto))
                served[0] = max(served[0], upto)

    def sibling_done(b, j, k):
        zz = (z + mp - k) % mp
        if b == 0:
            ref = wq.at[:, pl.ds(0, width // 2), pl.ds(0, cq)]
        elif b == 1:
            ref = wo.at[pl.ds(0, width // 2), pl.ds(0, cq)]
        else:
            ref = wholes[b].at[pl.ds(0, width // 2), pl.ds(0, hu)]
        pltpu.make_async_copy(ref, ref, sib_sem.at[piece(b, j), zz]).wait()

    def tokens(ref, block):
        return ref.at[pl.ds(pl.multiple_of(block * tok, tok), tok), :]

    def own_local(b):
        zz = z
        rows = pl.ds(pl.multiple_of(d * rb, rb), rb)
        if b == 0:
            dst = wq.at[:, rows, pl.ds(pl.multiple_of(zz * cq, 128), cq)]
        elif b == 1:
            dst = wo.at[rows, pl.ds(pl.multiple_of(zz * cq, 128), cq)]
        else:
            dst = wholes[b].at[rows, pl.ds(pl.multiple_of(zz * cu, 128), cu)]
        return pltpu.make_async_copy(shards[b], dst, local_sem.at[b])

    barrier = pltpu.get_barrier_semaphore()
    def flip(index, bit):
        return index + bit - 2 * bit * ((index // bit) % 2)

    peers = [(d, flip(z, 1 << s)) for s in range(mp.bit_length() - 1)]
    peers += [(flip(d, 1 << s), z) for s in range(1, dp.bit_length() - 1)] + [sibling]
    partners = [sibling, right, left] + [(d, (z + hop) % mp) for hop in range(1, mp)] + peers
    for target in partners:
        pl.semaphore_signal(barrier, inc=1, device_id=target, device_id_type=MESH)
    for b in range(4):
        own_local(b).start()
    own_hid = pltpu.make_async_copy(hid.at[z], tokens(xh, z), local_sem.at[4])
    own_cot = pltpu.make_async_copy(cot.at[z], tokens(ct, z), local_sem.at[5])
    own_hid.start()
    own_cot.start()
    pl.semaphore_wait(barrier, len(partners))

    def exchange_in(src, dst, which, hop):
        there = (z + hop) % mp
        pltpu.make_async_remote_copy(
            src_ref=src.at[there], dst_ref=tokens(dst, z), send_sem=row_send.at[which, there],
            recv_sem=row_recv.at[which, z], device_id=(d, there), device_id_type=MESH,
        ).start()

    def exchange_wait(src, dst, which):
        for hop in range(1, mp):
            there = (z + hop) % mp
            pltpu.make_async_copy(tokens(dst, there), tokens(dst, there), row_recv.at[which, there]).wait()

    def sends_wait(ref, which):
        for hop in range(1, mp):
            there = (z + hop) % mp
            pltpu.make_async_copy(ref, ref, row_send.at[which, there]).wait()

    column_out(0)
    for p, (b, j) in enumerate(pieces):
        start_own(b, j)

    serve_to(whole_at(0, 0, mp - 1))
    own_hid.wait()
    exchange_wait(hid, xh, 0)
    length = lens[z]
    separator = seps[z]
    seg0 = seg[0:1, :]
    seg_step = seg[1:2, :] - seg[0:1, :]

    def embed(rows, first):
        at = lax.broadcasted_iota(jnp.int32, (ROWS, 1), 0) + first
        flag = jnp.where(at > separator, 1.0, 0.0).astype(F32)
        return xh[rows, :].astype(F32) + seg0 + flag * seg_step

    @pl.loop(0, seq // ROWS)
    def _(i):
        first = pl.multiple_of(i * ROWS, ROWS)
        rows = pl.ds(first, ROWS)
        low[rows, :] = embed(rows, first).astype(BF16)

    own_local(0).wait()
    for k in range(mp):
        sibling_done(0, 0, k)

    tile = 256

    @pl.loop(0, width // tile)
    def _(i):
        base_t = whole_at(0, 0, mp - 1)
        serve_within(i, width // tile, lambda n: base_t + (n + 1) * QKV_TICKS // (width // tile))
        cols = pl.ds(pl.multiple_of(i * tile, tile), tile)
        qs[:, cols] = ((dot(low[...], wq[0, :, cols]) + bias_q[:, cols]) * scale).astype(BF16)
        ks[:, cols] = dot(low[...], wq[1, :, cols]).astype(BF16)
        vs[:, cols] = (dot(low[...], wq[2, :, cols]) + bias_v[:, cols]).astype(BF16)

    pairs = heads // 2
    lane = lax.broadcasted_iota(jnp.int32, (seq, 2 * HEAD_DIM), 1)

    def half_of(x, hh):
        keep = lane < HEAD_DIM if hh == 0 else lane >= HEAD_DIM
        return jnp.where(keep, x, jnp.zeros_like(x))

    items = 2 * mp

    @pl.loop(0, pairs)
    def _(i):
        base_t = whole_at(0, 0, mp - 1) + QKV_TICKS
        serve_within(i, pairs, lambda n: base_t + (n + 1) * ATTN_TICKS // pairs)
        cols = pl.ds(pl.multiple_of(i * 128, 128), 128)
        q2 = qs[:, cols]
        k2 = ks[:, cols]
        v2t = vs[:, cols].T
        ctxs = []
        for hh in range(2):
            st = dot(half_of(k2, hh), q2, NT)
            valid = lax.broadcasted_iota(jnp.int32, st.shape, 0) < length
            st = jnp.where(valid, st, -1e30)
            e = jnp.exp(st - jnp.max(st, axis=0, keepdims=True))
            p = (e * (1.0 / jnp.sum(e, axis=0, keepdims=True))).astype(BF16)
            probs[2 * i + hh] = p
            ctxs.append(dot(v2t[hh * HEAD_DIM:(hh + 1) * HEAD_DIM], p))
        low[:, cols] = jnp.concatenate(ctxs, axis=0).T.astype(BF16)

    own_local(1).wait()
    serve_to(whole_at(1, 0, mp - 1))
    for k in range(mp):
        sibling_done(1, 0, k)

    @pl.loop(0, width // tile)
    def _(i):
        cols = pl.ds(pl.multiple_of(i * tile, tile), tile)
        acc[:, cols] = dot(low[...], wo[cols, :], NT)

    @pl.loop(0, seq // ROWS)
    def _(i):
        first = pl.multiple_of(i * ROWS, ROWS)
        rows = pl.ds(first, ROWS)
        x = embed(rows, first) + acc[rows, :] + bias_out[...]
        center = x - row_mean(x)
        inv = lax.rsqrt(row_mean(center * center) + EPS)
        norm = center * inv
        normal[rows, :] = norm
        inverse[rows, :] = jnp.broadcast_to(inv, (ROWS, 128))
        low[rows, :] = (norm * gain_attn[...] + shift_attn[...]).astype(BF16)
        acc[rows, :] = jnp.zeros((ROWS, width), F32)

    own_local(2).wait()
    AFTER_ATTN = served[0]

    def slab(i):
        zz = (z + mp - i % mp) % mp
        return pl.multiple_of(zz * cu + (i // mp) * hu, 128)

    @pl.loop(0, items)
    def _(i):
        serve_within(i, items, lambda n: max(whole_at(2, n // mp, n % mp), AFTER_ATTN + (n + 1) * UP_TICKS // items))
        sibling_done(2, i // mp, i % mp)
        base = slab(i)

        @pl.loop(0, hu // tile)
        def _(n):
            cols = pl.ds(pl.multiple_of(base + n * tile, 128), tile)
            inner = dot(low[...], wu[:, cols]) + expand_bias[:, cols]
            cdf = 0.5 * (1.0 + lax.erf(inner * math.sqrt(0.5)))
            act[:, cols] = (inner * cdf).astype(BF16)
            bell = jnp.exp(-0.5 * inner * inner) * (1.0 / math.sqrt(2.0 * math.pi))
            slope[:, cols] = (cdf + inner * bell).astype(BF16)

    own_local(3).wait()

    @pl.loop(0, items)
    def _(i):
        serve_within(i, items, lambda n: max(whole_at(3, n // mp, n % mp), whole_at(3, 0, mp - 1) + n + 1))
        sibling_done(3, i // mp, i % mp)
        cols = pl.ds(slab(i), hu)

        @pl.loop(0, width // 512)
        def _(n):
            rows = pl.ds(pl.multiple_of(n * 512, 512), 512)
            acc[:, rows] += dot(act[:, cols], wd[rows, cols], NT)

    own_cot.wait()
    exchange_wait(cot, ct, 1)
    early[0] = jnp.zeros(early.shape[1:], F32)
    late[0] = jnp.zeros(late.shape[1:], F32)

    @pl.loop(0, seq // ROWS)
    def _(i):
        rows = pl.ds(pl.multiple_of(i * ROWS, ROWS), ROWS)
        x = normal[rows, :] * gain_attn[...] + shift_attn[...] + acc[rows, :] + bias_down[...]
        center = x - row_mean(x)
        inv = lax.rsqrt(row_mean(center * center) + EPS)
        norm = center * inv
        outb[rows, :] = (norm * gain_ffn[...] + shift_ffn[...]).astype(BF16)
        dy = ct[rows, :].astype(F32)
        e = dy * gain_ffn[...]
        g = inv * (e - row_mean(e) - norm * row_mean(e * norm))
        acc[rows, :] = g
        low[rows, :] = g.astype(BF16)
        early[0, 0:1, :] += jnp.sum(dy, axis=0, keepdims=True)
        early[0, 1:2, :] += jnp.sum(g, axis=0, keepdims=True)

    def push_out(buf, dst, which, there):
        pltpu.make_async_remote_copy(
            src_ref=tokens(buf, there), dst_ref=dst.at[z], send_sem=row_send.at[which, there],
            recv_sem=row_recv.at[which, z], device_id=(d, there), device_id_type=MESH,
        ).start()

    for hop in range(1, mp):
        push_out(outb, out, 2, (z + hop) % mp)
    keep_out = pltpu.make_async_copy(tokens(outb, z), out.at[z], local_sem.at[6])
    keep_out.start()

    for part in range(units // width):

        @pl.loop(0, width // tile)
        def _(i):
            here = pl.ds(pl.multiple_of(i * tile, tile), tile)
            cols = pl.ds(pl.multiple_of(part * width + i * tile, tile), tile)
            g = (dot(low[...], wd[:, cols]) * slope[:, cols].astype(F32)).astype(BF16)
            act[:, cols] = g
            early[0, 4 + part:5 + part, here] = jnp.sum(g.astype(F32), axis=0, keepdims=True)

    @pl.loop(0, width // tile)
    def _(i):
        cols = pl.ds(pl.multiple_of(i * tile, tile), tile)
        acc[:, cols] += dot(act[...], wu[cols, :], NT)

    @pl.loop(0, seq // ROWS)
    def _(i):
        rows = pl.ds(pl.multiple_of(i * ROWS, ROWS), ROWS)
        g = acc[rows, :]
        norm = normal[rows, :]
        e = g * gain_attn[...]
        first = inverse[rows, 0:1] * (e - row_mean(e) - norm * row_mean(e * norm))
        acc[rows, :] = first
        low[rows, :] = first.astype(BF16)
        early[0, 2:3, :] += jnp.sum(g, axis=0, keepdims=True)
        early[0, 3:4, :] += jnp.sum(first, axis=0, keepdims=True)

    @pl.loop(0, width // tile)
    def _(i):
        cols = pl.ds(pl.multiple_of(i * tile, tile), tile)
        gctx[:, cols] = dot(low[...], wo[:, cols]).astype(BF16)

    def sum_send_step(buf, which, s):
        pltpu.make_async_remote_copy(
            src_ref=buf.at[s], dst_ref=inbox.at[which, s], send_sem=sum_send.at[which, s],
            recv_sem=sum_recv.at[which, s], device_id=peers[s], device_id_type=MESH,
        ).start()

    def sum_take_step(buf, which, s):
        pltpu.make_async_copy(inbox.at[which, s], inbox.at[which, s], sum_recv.at[which, s]).wait()
        buf[s + 1] = buf[s] + inbox[which, s]

    steps = len(peers)
    sum_send_step(early, 0, 0)

    @pl.loop(0, pairs)
    def _(i):
        for s in range(steps):

            @pl.when(i == min(s + 1, pairs - 1))
            def _(s=s):
                sum_take_step(early, 0, s)
                if s + 1 < steps:
                    sum_send_step(early, 0, s + 1)

        cols = pl.ds(pl.multiple_of(i * 128, 128), 128)
        q2 = qs[:, cols]
        k2t = ks[:, cols].T
        v2 = vs[:, cols]
        g2 = gctx[:, cols]
        dq, dk, dv = [], [], []
        for hh in range(2):
            p = probs[2 * i + hh]
            pf = p.astype(F32)
            dpt = dot(half_of(v2, hh), g2, NT)
            ds = (pf * (dpt - jnp.sum(pf * dpt, axis=0, keepdims=True))).astype(BF16)
            dk.append(dot(ds, q2))
            dv.append(dot(p, g2))
            dq.append(dot(k2t[hh * HEAD_DIM:(hh + 1) * HEAD_DIM], ds))
        dq2 = jnp.concatenate(dq, axis=0).T.astype(BF16).astype(F32) * scale
        dv2 = jnp.where(lane < HEAD_DIM, dv[0], dv[1]).astype(BF16)
        qs[:, cols] = dq2.astype(BF16)
        ks[:, cols] = jnp.where(lane < HEAD_DIM, dk[0], dk[1]).astype(BF16)
        vs[:, cols] = dv2
        late[0, 0:1, cols] = jnp.sum(dq2, axis=0, keepdims=True)
        late[0, 1:2, cols] = jnp.sum(dv2.astype(F32), axis=0, keepdims=True)

    sum_send_step(late, 1, 0)
    side = seq // 2
    per = mp // 2
    mine = z // per
    for turn in range(2):
        block = 1 - mine if turn == 0 else mine
        rows = pl.ds(pl.multiple_of(block * side, side), side)

        @pl.loop(0, width // tile)
        def _(i):
            for u in range(2):
                s = 2 * turn + u

                @pl.when(i == 2 * u + 1)
                def _(s=s):
                    sum_take_step(late, 1, s)
                    sum_send_step(late, 1, s + 1)

            cols = pl.ds(pl.multiple_of(i * tile, tile), tile)
            x = acc[rows, cols]
            x += dot(qs[rows, :], wq[0, cols, :], NT)
            x += dot(ks[rows, :], wq[1, cols, :], NT)
            x += dot(vs[rows, :], wq[2, cols, :], NT)
            xh[rows, cols] = x.astype(BF16)

        for q in range(per):
            there = block * per + (z + q + turn) % per
            if turn == 0 or q < per - 1:
                push_out(xh, grad, 3, there)
    keep_grad = pltpu.make_async_copy(tokens(xh, z), grad.at[z], local_sem.at[7])
    keep_grad.start()

    for s in range(4, steps):
        sum_take_step(late, 1, s)
        if s + 1 < steps:
            sum_send_step(late, 1, s + 1)
    sums[0] = early[steps]
    sums[1] = late[steps]
    for which, buf in ((0, early), (1, late)):
        for s in range(steps):
            pltpu.make_async_copy(buf.at[s], buf.at[s], sum_send.at[which, s]).wait()

    keep_out.wait()
    keep_grad.wait()
    for which, src in ((0, tokens(xh, z)), (1, tokens(xh, z)), (2, tokens(xh, z)), (3, tokens(xh, z))):
        sends_wait(src, which)
    for which, ref in ((2, out), (3, grad)):
        for hop in range(1, mp):
            there = (z + hop) % mp
            pltpu.make_async_copy(ref.at[there], ref.at[there], row_recv.at[which, there]).wait()
    for b in range(4):
        ref = wholes[b]
        cols = (cq if b < 2 else cu) * mp
        ways = (
            (rb * (2 * half - 1), cols // 2),
            (rb * (2 * half - 1), cols // 2),
            (width // 2, cols),
            (rb, cols - cols // mp),
        )
        for way, (r, c) in enumerate(ways):
            part = ref.at[:, pl.ds(0, r), pl.ds(0, c)] if b == 0 else ref.at[pl.ds(0, r), pl.ds(0, c)]
            pltpu.make_async_copy(part, part, send_sem.at[b, way]).wait()


def on_device(
    hidden_in, lengths, separators, seg_table, query_key_value_weight, output_weight, up_weight, down_weight,
    bias_q, bias_v, bias_out, expand_bias, bias_down, gain_attn, shift_attn, gain_ffn, shift_ffn, cotangent,
):
    dp, mp = lax.axis_size("dp"), lax.axis_size("mp")
    here, tok, width = hidden_in.shape
    assert here == mp
    seq = tok * mp
    units = up_weight.shape[1] * mp
    heads = width // HEAD_DIM
    vmem = pl.BlockSpec(memory_space=pltpu.VMEM)
    smem = pl.BlockSpec(memory_space=pltpu.SMEM)
    anys = pl.BlockSpec(memory_space=pl.ANY)
    rows = [seg_table] + [
        v.reshape(1, -1)
        for v in (bias_q, bias_v, bias_out, expand_bias, bias_down, gain_attn, shift_attn, gain_ffn, shift_ffn)
    ]
    steps = dp.bit_length() + mp.bit_length() - 2
    summed = (4 + units // width, width)
    moved = jax.ShapeDtypeStruct(hidden_in.shape, BF16)
    ring = dp // 2
    sem = pltpu.SemaphoreType.DMA
    results = pl.pallas_call(
        functools.partial(step_kernel, (dp, mp, seq, width, units)),
        name="step",
        out_shape=(moved, moved, jax.ShapeDtypeStruct((2,) + summed, F32)),
        in_specs=[smem, smem] + [vmem] * 10 + [anys] * 6,
        out_specs=(anys, anys, vmem),
        scratch_shapes=[
            pltpu.VMEM((3, width, width), BF16),
            pltpu.VMEM((width, width), BF16),
            pltpu.VMEM((width, units), BF16),
            pltpu.VMEM((width, units), BF16),
            *[pltpu.VMEM((seq, width), BF16)] * 7,
            pltpu.VMEM((heads, seq, seq), BF16),
            pltpu.VMEM((seq, width), F32),
            pltpu.VMEM((seq, 128), F32),
            pltpu.VMEM((seq, width), F32),
            pltpu.VMEM((seq, units), BF16),
            pltpu.VMEM((seq, units), BF16),
            pltpu.VMEM((seq, width), BF16),
            pltpu.VMEM((steps + 1,) + summed, F32),
            pltpu.VMEM((steps + 1,) + summed, F32),
            pltpu.VMEM((2, steps) + summed, F32),
            sem((8,)),
            sem((6, mp, ring)),
            sem((6, mp)),
            sem((4, 4)),
            sem((4, mp)),
            sem((4, mp)),
            sem((2, steps)),
            sem((2, steps)),
        ],
        compiler_params=pltpu.CompilerParams(collective_id=0, has_side_effects=True, vmem_limit_bytes=67043328),
    )(
        lengths, separators, *rows, hidden_in, cotangent, jnp.swapaxes(query_key_value_weight, 0, 1),
        output_weight, up_weight, down_weight,
    )
    sums = results[2] * (1.0 / (here * seq * dp))
    first, last = sums[0], sums[1]
    return results[:2] + (last[0], last[1], first[3], first[4:].reshape(-1), first[1], first[2], first[0])


def solution(mesh):
    rows = P("dp", "mp", None)
    frozen = P("dp", "mp")
    placed = (rows, P("dp"), P("dp"), P(), P("dp", None, "mp"), frozen, frozen, frozen) + (P(),) * 9 + (rows,)
    return jax.shard_map(on_device, mesh=mesh, in_specs=placed, out_specs=(rows, rows) + (P(),) * 7, check_vma=False)
```

```python
import functools
import math

import jax
import jax.numpy as jnp
from jax import lax
from jax.experimental import pallas as pl
from jax.experimental.pallas import tpu as pltpu
from jax.sharding import PartitionSpec as P

HEAD_DIM = 64
EPS = 1e-12
F32 = jnp.float32
BF16 = jnp.bfloat16
MESH = pl.DeviceIdType.MESH
ROWS = 64
LAG = 0
PLAN = {0: (1,), 3: (2,), 6: (3,), 9: (4,), 12: (5,)}
HID_AT = {1: (1,2,3)}
COT_AT = {16: (1,2,3)}
QKV_TICKS = 2
ATTN_TICKS = 4
UP_TICKS = 6
NN = ((1,), (0,))
NT = ((1,), (1,))


def dot(a, b, dims=NN):
    return lax.dot_general(a, b, (dims, ((), ())), preferred_element_type=F32)


def snake(pos):
    high = pos // 2
    return 2 * high + (pos % 2 + high) % 2


def row_mean(x):
    return jnp.sum(x, axis=-1, keepdims=True) * (1.0 / x.shape[-1])


def step_kernel(
    shape, lens, seps, seg, bias_q, bias_v, bias_out, expand_bias, bias_down, gain_attn, shift_attn, gain_ffn,
    shift_ffn, hid, cot, wq_in, wo_in, wu_in, wd_in,
    out, grad, sums,
    wq, wo, wu, wd, xh, ct, outb, low, qs, ks, vs, probs, normal, inverse, acc, act, slope, gctx,
    early, late, inbox, local_sem, ici_sem, sib_sem, send_sem, row_recv, row_send, sum_recv, sum_send,
):
    dp, mp, seq, width, units = shape
    ring, half = dp // 2, dp // 4
    rb = width // dp
    cq = width // mp
    cu = units // mp
    hu = cu // 2
    tok = seq // mp
    heads = width // HEAD_DIM
    scale = 1.0 / math.sqrt(HEAD_DIM)
    d = lax.axis_index("dp")
    z = lax.axis_index("mp")
    core = d % 2
    pos = snake(d // 2)
    right = (2 * snake((pos + 1) % ring) + core, z)
    left = (2 * snake((pos + ring - 1) % ring) + core, z)
    sibling = (d + 1 - 2 * core, z)
    wholes = (wq, wo, wu, wd)
    shards = (wq_in, wo_in, wu_in, wd_in)

    def region(b, j, k, origin):
        zz = (z + mp - k) % mp
        rows = pl.ds(pl.multiple_of((2 * snake(origin) + core) * rb, rb), rb)
        if b == 0:
            return wq.at[:, rows, pl.ds(pl.multiple_of(zz * cq, 128), cq)]
        if b == 1:
            return wo.at[rows, pl.ds(pl.multiple_of(zz * cq, 128), cq)]
        return wholes[b].at[rows, pl.ds(pl.multiple_of(zz * cu + j * hu, 128), hu)]

    def own_shard(b, j):
        if b < 2:
            return shards[b]
        return shards[b].at[:, pl.ds(pl.multiple_of(j * hu, 128), hu)]

    def piece(b, j):
        return (0, 1, 2, 4)[b] + j

    def send(src, b, j, k, origin, way, target, part=()):
        zz = (z + mp - k) % mp
        dst = region(b, j, k, origin).at[part] if part else region(b, j, k, origin)
        recv = sib_sem.at[piece(b, j), zz] if way == 2 else ici_sem.at[piece(b, j), zz, origin]
        pltpu.make_async_remote_copy(
            src_ref=src, dst_ref=dst, send_sem=send_sem.at[b, way], recv_sem=recv, device_id=target, device_id_type=MESH
        ).start()

    def arrived(b, j, k, origin):
        zz = (z + mp - k) % mp
        ref = region(b, j, k, origin)
        pltpu.make_async_copy(ref, ref, ici_sem.at[piece(b, j), zz, origin]).wait()
        return ref

    def spread(src, b, j, k):
        send(src, b, j, k, pos, 0, right)
        send(src, b, j, k, pos, 1, left)
        send(src, b, j, k, pos, 2, sibling)

    def start_own(b, j):
        spread(own_shard(b, j), b, j, 0)

    def send_z(b, j, there):
        pltpu.make_async_remote_copy(
            src_ref=own_shard(b, j), dst_ref=region(b, j, 0, pos), send_sem=send_sem.at[b, 3],
            recv_sem=ici_sem.at[piece(b, j), z, pos], device_id=(d, there), device_id_type=MESH,
        ).start()

    def serve_column(b, j, k):
        spread(arrived(b, j, k, pos), b, j, k)

    def pick(cond, fn):
        if isinstance(cond, bool):
            if cond:
                fn()
        else:
            pl.when(cond)(fn)

    def relay(ref, b, j, k, origin, way, target):
        part = (slice(None),) * (b == 0) + (pl.ds(way * (rb // 2), rb // 2),)
        send(ref.at[part], b, j, k, origin, way, target, part)

    def serve_ring(b, j, k, dist):
        if dist == half:
            origin = (pos + half) % ring
            send(arrived(b, j, k, origin), b, j, k, origin, 2, sibling)
            return
        pass_on = relay if dist + 1 == half else send
        for way, origin, target in ((0, (pos + ring - dist) % ring, right), (1, (pos + dist) % ring, left)):
            ref = arrived(b, j, k, origin)
            pass_on(ref, b, j, k, origin, way, target)
            send(ref, b, j, k, origin, 2, sibling)

    pieces = ((0, 0), (1, 0), (2, 0), (2, 1), (3, 0), (3, 1))
    order = [(b, j, 0) for b, j in pieces] + [(b, j, k) for b, j in pieces for k in range(1, mp)]
    lag = half + LAG
    served = [0]

    def with_item(t, fn):
        if 0 <= t < len(order):
            fn(*order[t])

    def tick(t):
        with_item(t, lambda b, j, k: k > 0 and serve_column(b, j, k))
        for dist in range(1, half + 1):
            with_item(t - dist - LAG, lambda b, j, k: serve_ring(b, j, k, dist))

    def column_out(p):
        for hop in range(1, mp):
            send_z(*pieces[p], (z + hop) % mp)

    def serve_to(count):
        for t in range(served[0], count):
            for p in PLAN.get(t, ()):
                column_out(p)
            for hop in HID_AT.get(t, ()):
                exchange_in(hid, xh, 0, hop)
            for hop in COT_AT.get(t, ()):
                exchange_in(cot, ct, 1, hop)
            tick(t)
        served[0] = max(served[0], count)

    def whole_at(b, j, k):
        return order.index((b, j, k)) + lag + 1

    def serve_within(i, slots, until):
        first = served[0]
        for slot in range(slots):
            upto = min(until(slot), len(order) + lag)
            if upto > served[0]:
                pl.when(i == slot)(functools.partial(serve_to, upto))
                served[0] = max(served[0], upto)

    def sibling_done(b, j, k):
        zz = (z + mp - k) % mp
        if b == 0:
            ref = wq.at[:, pl.ds(0, width // 2), pl.ds(0, cq)]
        elif b == 1:
            ref = wo.at[pl.ds(0, width // 2), pl.ds(0, cq)]
        else:
            ref = wholes[b].at[pl.ds(0, width // 2), pl.ds(0, hu)]
        pltpu.make_async_copy(ref, ref, sib_sem.at[piece(b, j), zz]).wait()

    def tokens(ref, block):
        return ref.at[pl.ds(pl.multiple_of(block * tok, tok), tok), :]

    def own_local(b):
        zz = z
        rows = pl.ds(pl.multiple_of(d * rb, rb), rb)
        if b == 0:
            dst = wq.at[:, rows, pl.ds(pl.multiple_of(zz * cq, 128), cq)]
        elif b == 1:
            dst = wo.at[rows, pl.ds(pl.multiple_of(zz * cq, 128), cq)]
        else:
            dst = wholes[b].at[rows, pl.ds(pl.multiple_of(zz * cu, 128), cu)]
        return pltpu.make_async_copy(shards[b], dst, local_sem.at[b])

    barrier = pltpu.get_barrier_semaphore()
    def flip(index, bit):
        return index + bit - 2 * bit * ((index // bit) % 2)

    peers = [(d, flip(z, 1 << s)) for s in range(mp.bit_length() - 1)]
    peers += [(flip(d, 1 << s), z) for s in range(1, dp.bit_length() - 1)] + [sibling]
    partners = [sibling, right, left] + [(d, (z + hop) % mp) for hop in range(1, mp)] + peers
    for target in partners:
        pl.semaphore_signal(barrier, inc=1, device_id=target, device_id_type=MESH)
    for b in range(4):
        own_local(b).start()
    own_hid = pltpu.make_async_copy(hid.at[z], tokens(xh, z), local_sem.at[4])
    own_cot = pltpu.make_async_copy(cot.at[z], tokens(ct, z), local_sem.at[5])
    own_hid.start()
    own_cot.start()
    pl.semaphore_wait(barrier, len(partners))

    def exchange_in(src, dst, which, hop):
        there = (z + hop) % mp
        pltpu.make_async_remote_copy(
            src_ref=src.at[there], dst_ref=tokens(dst, z), send_sem=row_send.at[which, there],
            recv_sem=row_recv.at[which, z], device_id=(d, there), device_id_type=MESH,
        ).start()

    def exchange_wait(src, dst, which):
        for hop in range(1, mp):
            there = (z + hop) % mp
            pltpu.make_async_copy(tokens(dst, there), tokens(dst, there), row_recv.at[which, there]).wait()

    def sends_wait(ref, which):
        for hop in range(1, mp):
            there = (z + hop) % mp
            pltpu.make_async_copy(ref, ref, row_send.at[which, there]).wait()

    column_out(0)
    for p, (b, j) in enumerate(pieces):
        start_own(b, j)

    serve_to(whole_at(0, 0, mp - 1))
    own_hid.wait()
    exchange_wait(hid, xh, 0)
    length = lens[z]
    separator = seps[z]
    seg0 = seg[0:1, :]
    seg_step = seg[1:2, :] - seg[0:1, :]

    def embed(rows, first):
        at = lax.broadcasted_iota(jnp.int32, (ROWS, 1), 0) + first
        flag = jnp.where(at > separator, 1.0, 0.0).astype(F32)
        return xh[rows, :].astype(F32) + seg0 + flag * seg_step

    @pl.loop(0, seq // ROWS)
    def _(i):
        first = pl.multiple_of(i * ROWS, ROWS)
        rows = pl.ds(first, ROWS)
        low[rows, :] = embed(rows, first).astype(BF16)

    own_local(0).wait()
    for k in range(mp):
        sibling_done(0, 0, k)

    tile = 256

    @pl.loop(0, width // tile)
    def _(i):
        base_t = whole_at(0, 0, mp - 1)
        serve_within(i, width // tile, lambda n: base_t + (n + 1) * QKV_TICKS // (width // tile))
        cols = pl.ds(pl.multiple_of(i * tile, tile), tile)
        qs[:, cols] = ((dot(low[...], wq[0, :, cols]) + bias_q[:, cols]) * scale).astype(BF16)
        ks[:, cols] = dot(low[...], wq[1, :, cols]).astype(BF16)
        vs[:, cols] = (dot(low[...], wq[2, :, cols]) + bias_v[:, cols]).astype(BF16)

    pairs = heads // 2
    lane = lax.broadcasted_iota(jnp.int32, (seq, 2 * HEAD_DIM), 1)

    def half_of(x, hh):
        keep = lane < HEAD_DIM if hh == 0 else lane >= HEAD_DIM
        return jnp.where(keep, x, jnp.zeros_like(x))

    items = 2 * mp

    @pl.loop(0, pairs)
    def _(i):
        base_t = whole_at(0, 0, mp - 1) + QKV_TICKS
        serve_within(i, pairs, lambda n: base_t + (n + 1) * ATTN_TICKS // pairs)
        cols = pl.ds(pl.multiple_of(i * 128, 128), 128)
        q2 = qs[:, cols]
        k2 = ks[:, cols]
        v2t = vs[:, cols].T
        ctxs = []
        for hh in range(2):
            st = dot(half_of(k2, hh), q2, NT)
            valid = lax.broadcasted_iota(jnp.int32, st.shape, 0) < length
            st = jnp.where(valid, st, -1e30)
            e = jnp.exp(st - jnp.max(st, axis=0, keepdims=True))
            p = (e * (1.0 / jnp.sum(e, axis=0, keepdims=True))).astype(BF16)
            probs[2 * i + hh] = p
            ctxs.append(dot(v2t[hh * HEAD_DIM:(hh + 1) * HEAD_DIM], p))
        low[:, cols] = jnp.concatenate(ctxs, axis=0).T.astype(BF16)

    own_local(1).wait()
    serve_to(whole_at(1, 0, mp - 1))
    for k in range(mp):
        sibling_done(1, 0, k)

    @pl.loop(0, width // tile)
    def _(i):
        cols = pl.ds(pl.multiple_of(i * tile, tile), tile)
        acc[:, cols] = dot(low[...], wo[cols, :], NT)

    @pl.loop(0, seq // ROWS)
    def _(i):
        first = pl.multiple_of(i * ROWS, ROWS)
        rows = pl.ds(first, ROWS)
        x = embed(rows, first) + acc[rows, :] + bias_out[...]
        center = x - row_mean(x)
        inv = lax.rsqrt(row_mean(center * center) + EPS)
        norm = center * inv
        normal[rows, :] = norm
        inverse[rows, :] = jnp.broadcast_to(inv, (ROWS, 128))
        low[rows, :] = (norm * gain_attn[...] + shift_attn[...]).astype(BF16)
        acc[rows, :] = jnp.zeros((ROWS, width), F32)

    own_local(2).wait()
    AFTER_ATTN = served[0]

    def slab(i):
        zz = (z + mp - i % mp) % mp
        return pl.multiple_of(zz * cu + (i // mp) * hu, 128)

    @pl.loop(0, items)
    def _(i):
        serve_within(i, items, lambda n: max(whole_at(2, n // mp, n % mp), AFTER_ATTN + (n + 1) * UP_TICKS // items))
        sibling_done(2, i // mp, i % mp)
        base = slab(i)

        @pl.loop(0, hu // tile)
        def _(n):
            cols = pl.ds(pl.multiple_of(base + n * tile, 128), tile)
            inner = dot(low[...], wu[:, cols]) + expand_bias[:, cols]
            cdf = 0.5 * (1.0 + lax.erf(inner * math.sqrt(0.5)))
            act[:, cols] = (inner * cdf).astype(BF16)
            bell = jnp.exp(-0.5 * inner * inner) * (1.0 / math.sqrt(2.0 * math.pi))
            slope[:, cols] = (cdf + inner * bell).astype(BF16)

    own_local(3).wait()

    @pl.loop(0, items)
    def _(i):
        serve_within(i, items, lambda n: max(whole_at(3, n // mp, n % mp), whole_at(3, 0, mp - 1) + n + 1))
        sibling_done(3, i // mp, i % mp)
        cols = pl.ds(slab(i), hu)

        @pl.loop(0, width // 512)
        def _(n):
            rows = pl.ds(pl.multiple_of(n * 512, 512), 512)
            acc[:, rows] += dot(act[:, cols], wd[rows, cols], NT)

    own_cot.wait()
    exchange_wait(cot, ct, 1)
    early[0] = jnp.zeros(early.shape[1:], F32)
    late[0] = jnp.zeros(late.shape[1:], F32)

    @pl.loop(0, seq // ROWS)
    def _(i):
        rows = pl.ds(pl.multiple_of(i * ROWS, ROWS), ROWS)
        x = normal[rows, :] * gain_attn[...] + shift_attn[...] + acc[rows, :] + bias_down[...]
        center = x - row_mean(x)
        inv = lax.rsqrt(row_mean(center * center) + EPS)
        norm = center * inv
        outb[rows, :] = (norm * gain_ffn[...] + shift_ffn[...]).astype(BF16)
        dy = ct[rows, :].astype(F32)
        e = dy * gain_ffn[...]
        g = inv * (e - row_mean(e) - norm * row_mean(e * norm))
        acc[rows, :] = g
        low[rows, :] = g.astype(BF16)
        early[0, 0:1, :] += jnp.sum(dy, axis=0, keepdims=True)
        early[0, 1:2, :] += jnp.sum(g, axis=0, keepdims=True)

    def push_out(buf, dst, which, there):
        pltpu.make_async_remote_copy(
            src_ref=tokens(buf, there), dst_ref=dst.at[z], send_sem=row_send.at[which, there],
            recv_sem=row_recv.at[which, z], device_id=(d, there), device_id_type=MESH,
        ).start()

    for hop in range(1, mp):
        push_out(outb, out, 2, (z + hop) % mp)
    keep_out = pltpu.make_async_copy(tokens(outb, z), out.at[z], local_sem.at[6])
    keep_out.start()

    for part in range(units // width):

        @pl.loop(0, width // tile)
        def _(i):
            here = pl.ds(pl.multiple_of(i * tile, tile), tile)
            cols = pl.ds(pl.multiple_of(part * width + i * tile, tile), tile)
            g = (dot(low[...], wd[:, cols]) * slope[:, cols].astype(F32)).astype(BF16)
            act[:, cols] = g
            early[0, 4 + part:5 + part, here] = jnp.sum(g.astype(F32), axis=0, keepdims=True)

    @pl.loop(0, width // tile)
    def _(i):
        cols = pl.ds(pl.multiple_of(i * tile, tile), tile)
        acc[:, cols] += dot(act[...], wu[cols, :], NT)

    @pl.loop(0, seq // ROWS)
    def _(i):
        rows = pl.ds(pl.multiple_of(i * ROWS, ROWS), ROWS)
        g = acc[rows, :]
        norm = normal[rows, :]
        e = g * gain_attn[...]
        first = inverse[rows, 0:1] * (e - row_mean(e) - norm * row_mean(e * norm))
        acc[rows, :] = first
        low[rows, :] = first.astype(BF16)
        early[0, 2:3, :] += jnp.sum(g, axis=0, keepdims=True)
        early[0, 3:4, :] += jnp.sum(first, axis=0, keepdims=True)

    @pl.loop(0, width // tile)
    def _(i):
        cols = pl.ds(pl.multiple_of(i * tile, tile), tile)
        gctx[:, cols] = dot(low[...], wo[:, cols]).astype(BF16)

    def sum_send_step(buf, which, s):
        pltpu.make_async_remote_copy(
            src_ref=buf.at[s], dst_ref=inbox.at[which, s], send_sem=sum_send.at[which, s],
            recv_sem=sum_recv.at[which, s], device_id=peers[s], device_id_type=MESH,
        ).start()

    def sum_take_step(buf, which, s):
        pltpu.make_async_copy(inbox.at[which, s], inbox.at[which, s], sum_recv.at[which, s]).wait()
        buf[s + 1] = buf[s] + inbox[which, s]

    def sum_pass(buf, which, s):
        if s < steps:
            sum_take_step(buf, which, s)
            if s + 1 < steps:
                sum_send_step(buf, which, s + 1)

    steps = len(peers)
    in_loop = min(steps, (pairs - 1) // 2)
    sum_send_step(early, 0, 0)

    @pl.loop(0, pairs)
    def _(i):
        for s in range(in_loop):

            @pl.when(i == 2 * s + 2)
            def _(s=s):
                sum_pass(early, 0, s)

        cols = pl.ds(pl.multiple_of(i * 128, 128), 128)
        q2 = qs[:, cols]
        k2t = ks[:, cols].T
        v2 = vs[:, cols]
        g2 = gctx[:, cols]
        dq, dk, dv = [], [], []
        for hh in range(2):
            p = probs[2 * i + hh]
            pf = p.astype(F32)
            dpt = dot(half_of(v2, hh), g2, NT)
            ds = (pf * (dpt - jnp.sum(pf * dpt, axis=0, keepdims=True))).astype(BF16)
            dk.append(dot(ds, q2))
            dv.append(dot(p, g2))
            dq.append(dot(k2t[hh * HEAD_DIM:(hh + 1) * HEAD_DIM], ds))
        dq2 = jnp.concatenate(dq, axis=0).T.astype(BF16).astype(F32) * scale
        dv2 = jnp.where(lane < HEAD_DIM, dv[0], dv[1]).astype(BF16)
        qs[:, cols] = dq2.astype(BF16)
        ks[:, cols] = jnp.where(lane < HEAD_DIM, dk[0], dk[1]).astype(BF16)
        vs[:, cols] = dv2
        late[0, 0:1, cols] = jnp.sum(dq2, axis=0, keepdims=True)
        late[0, 1:2, cols] = jnp.sum(dv2.astype(F32), axis=0, keepdims=True)

    sum_send_step(late, 1, 0)
    side = seq // 2
    per = mp // 2
    mine = z // per
    for turn in range(2):
        block = 1 - mine if turn == 0 else mine
        rows = pl.ds(pl.multiple_of(block * side, side), side)

        @pl.loop(0, width // tile)
        def _(i):
            cols = pl.ds(pl.multiple_of(i * tile, tile), tile)
            x = acc[rows, cols]
            x += dot(qs[rows, :], wq[0, cols, :], NT)
            x += dot(ks[rows, :], wq[1, cols, :], NT)
            x += dot(vs[rows, :], wq[2, cols, :], NT)
            xh[rows, cols] = x.astype(BF16)

        sum_pass(early, 0, in_loop + turn)
        sum_pass(late, 1, turn)
        for q in range(per):
            there = block * per + (z + q + turn) % per
            if turn == 0 or q < per - 1:
                push_out(xh, grad, 3, there)
    keep_grad = pltpu.make_async_copy(tokens(xh, z), grad.at[z], local_sem.at[7])
    keep_grad.start()

    for s in range(2, steps):
        sum_pass(early, 0, in_loop + s)
        sum_pass(late, 1, s)
    sums[0] = early[steps]
    sums[1] = late[steps]
    for which, buf in ((0, early), (1, late)):
        for s in range(steps):
            pltpu.make_async_copy(buf.at[s], buf.at[s], sum_send.at[which, s]).wait()

    keep_out.wait()
    keep_grad.wait()
    for which, src in ((0, tokens(xh, z)), (1, tokens(xh, z)), (2, tokens(xh, z)), (3, tokens(xh, z))):
        sends_wait(src, which)
    for which, ref in ((2, out), (3, grad)):
        for hop in range(1, mp):
            there = (z + hop) % mp
            pltpu.make_async_copy(ref.at[there], ref.at[there], row_recv.at[which, there]).wait()
    for b in range(4):
        ref = wholes[b]
        cols = (cq if b < 2 else cu) * mp
        ways = (
            (rb * (2 * half - 1), cols // 2),
            (rb * (2 * half - 1), cols // 2),
            (width // 2, cols),
            (rb, cols - cols // mp),
        )
        for way, (r, c) in enumerate(ways):
            part = ref.at[:, pl.ds(0, r), pl.ds(0, c)] if b == 0 else ref.at[pl.ds(0, r), pl.ds(0, c)]
            pltpu.make_async_copy(part, part, send_sem.at[b, way]).wait()


def on_device(
    hidden_in, lengths, separators, seg_table, query_key_value_weight, output_weight, up_weight, down_weight,
    bias_q, bias_v, bias_out, expand_bias, bias_down, gain_attn, shift_attn, gain_ffn, shift_ffn, cotangent,
):
    dp, mp = lax.axis_size("dp"), lax.axis_size("mp")
    here, tok, width = hidden_in.shape
    assert here == mp
    seq = tok * mp
    units = up_weight.shape[1] * mp
    heads = width // HEAD_DIM
    vmem = pl.BlockSpec(memory_space=pltpu.VMEM)
    smem = pl.BlockSpec(memory_space=pltpu.SMEM)
    anys = pl.BlockSpec(memory_space=pl.ANY)
    rows = [seg_table] + [
        v.reshape(1, -1)
        for v in (bias_q, bias_v, bias_out, expand_bias, bias_down, gain_attn, shift_attn, gain_ffn, shift_ffn)
    ]
    steps = dp.bit_length() + mp.bit_length() - 2
    summed = (4 + units // width, width)
    moved = jax.ShapeDtypeStruct(hidden_in.shape, BF16)
    ring = dp // 2
    sem = pltpu.SemaphoreType.DMA
    results = pl.pallas_call(
        functools.partial(step_kernel, (dp, mp, seq, width, units)),
        name="step",
        out_shape=(moved, moved, jax.ShapeDtypeStruct((2,) + summed, F32)),
        in_specs=[smem, smem] + [vmem] * 10 + [anys] * 6,
        out_specs=(anys, anys, vmem),
        scratch_shapes=[
            pltpu.VMEM((3, width, width), BF16),
            pltpu.VMEM((width, width), BF16),
            pltpu.VMEM((width, units), BF16),
            pltpu.VMEM((width, units), BF16),
            *[pltpu.VMEM((seq, width), BF16)] * 7,
            pltpu.VMEM((heads, seq, seq), BF16),
            pltpu.VMEM((seq, width), F32),
            pltpu.VMEM((seq, 128), F32),
            pltpu.VMEM((seq, width), F32),
            pltpu.VMEM((seq, units), BF16),
            pltpu.VMEM((seq, units), BF16),
            pltpu.VMEM((seq, width), BF16),
            pltpu.VMEM((steps + 1,) + summed, F32),
            pltpu.VMEM((steps + 1,) + summed, F32),
            pltpu.VMEM((2, steps) + summed, F32),
            sem((8,)),
            sem((6, mp, ring)),
            sem((6, mp)),
            sem((4, 4)),
            sem((4, mp)),
            sem((4, mp)),
            sem((2, steps)),
            sem((2, steps)),
        ],
        compiler_params=pltpu.CompilerParams(collective_id=0, has_side_effects=True, vmem_limit_bytes=67043328),
    )(
        lengths, separators, *rows, hidden_in, cotangent, jnp.swapaxes(query_key_value_weight, 0, 1),
        output_weight, up_weight, down_weight,
    )
    sums = results[2] * (1.0 / (here * seq * dp))
    first, last = sums[0], sums[1]
    return results[:2] + (last[0], last[1], first[3], first[4:].reshape(-1), first[1], first[2], first[0])


def solution(mesh):
    rows = P("dp", "mp", None)
    frozen = P("dp", "mp")
    placed = (rows, P("dp"), P("dp"), P(), P("dp", None, "mp"), frozen, frozen, frozen) + (P(),) * 9 + (rows,)
    return jax.shard_map(on_device, mesh=mesh, in_specs=placed, out_specs=(rows, rows) + (P(),) * 7, check_vma=False)
```

```python
import functools
import math

import jax
import jax.numpy as jnp
from jax import lax
from jax.experimental import pallas as pl
from jax.experimental.pallas import tpu as pltpu
from jax.sharding import PartitionSpec as P

HEAD_DIM = 64
EPS = 1e-12
F32 = jnp.float32
BF16 = jnp.bfloat16
MESH = pl.DeviceIdType.MESH
ROWS = 64
LAG = 0
PRE_TICKS = 13
PLAN = {0: (1,), 3: (2,), 6: (3,), 9: (4,), 12: (5,)}
HID_AT = {1: (1,2,3)}
COT_AT = {19: (1,2,3)}
ATTN_TICKS = 6
UP_TICKS = 6
NN = ((1,), (0,))
NT = ((1,), (1,))


def dot(a, b, dims=NN):
    return lax.dot_general(a, b, (dims, ((), ())), preferred_element_type=F32)


def snake(pos):
    high = pos // 2
    return 2 * high + (pos % 2 + high) % 2


def row_mean(x):
    return jnp.sum(x, axis=-1, keepdims=True) * (1.0 / x.shape[-1])


def step_kernel(
    shape, lens, seps, seg, bias_q, bias_v, bias_out, expand_bias, bias_down, gain_attn, shift_attn, gain_ffn,
    shift_ffn, hid, cot, wq_in, wo_in, wu_in, wd_in,
    out, grad, sums,
    wq, wo, wu, wd, xh, ct, outb, low, qs, ks, vs, probs, normal, inverse, acc, act, slope, gctx,
    early, late, inbox, local_sem, ici_sem, sib_sem, send_sem, row_recv, row_send, sum_recv, sum_send,
):
    dp, mp, seq, width, units = shape
    ring, half = dp // 2, dp // 4
    rb = width // dp
    cq = width // mp
    cu = units // mp
    hu = cu // 2
    tok = seq // mp
    heads = width // HEAD_DIM
    scale = 1.0 / math.sqrt(HEAD_DIM)
    d = lax.axis_index("dp")
    z = lax.axis_index("mp")
    core = d % 2
    pos = snake(d // 2)
    right = (2 * snake((pos + 1) % ring) + core, z)
    left = (2 * snake((pos + ring - 1) % ring) + core, z)
    sibling = (d + 1 - 2 * core, z)
    wholes = (wq, wo, wu, wd)
    shards = (wq_in, wo_in, wu_in, wd_in)

    def region(b, j, k, origin):
        zz = (z + mp - k) % mp
        rows = pl.ds(pl.multiple_of((2 * snake(origin) + core) * rb, rb), rb)
        if b == 0:
            return wq.at[:, rows, pl.ds(pl.multiple_of(zz * cq, 128), cq)]
        if b == 1:
            return wo.at[rows, pl.ds(pl.multiple_of(zz * cq, 128), cq)]
        return wholes[b].at[rows, pl.ds(pl.multiple_of(zz * cu + j * hu, 128), hu)]

    def own_shard(b, j):
        if b < 2:
            return shards[b]
        return shards[b].at[:, pl.ds(pl.multiple_of(j * hu, 128), hu)]

    def piece(b, j):
        return (0, 1, 2, 4)[b] + j

    def send(src, b, j, k, origin, way, target, part=()):
        zz = (z + mp - k) % mp
        dst = region(b, j, k, origin).at[part] if part else region(b, j, k, origin)
        recv = sib_sem.at[piece(b, j), zz] if way == 2 else ici_sem.at[piece(b, j), zz, origin]
        pltpu.make_async_remote_copy(
            src_ref=src, dst_ref=dst, send_sem=send_sem.at[b, way], recv_sem=recv, device_id=target, device_id_type=MESH
        ).start()

    def arrived(b, j, k, origin):
        zz = (z + mp - k) % mp
        ref = region(b, j, k, origin)
        pltpu.make_async_copy(ref, ref, ici_sem.at[piece(b, j), zz, origin]).wait()
        return ref

    def spread(src, b, j, k):
        send(src, b, j, k, pos, 0, right)
        send(src, b, j, k, pos, 1, left)
        send(src, b, j, k, pos, 2, sibling)

    def start_own(b, j):
        spread(own_shard(b, j), b, j, 0)

    def send_z(b, j, there):
        pltpu.make_async_remote_copy(
            src_ref=own_shard(b, j), dst_ref=region(b, j, 0, pos), send_sem=send_sem.at[b, 3],
            recv_sem=ici_sem.at[piece(b, j), z, pos], device_id=(d, there), device_id_type=MESH,
        ).start()

    def serve_column(b, j, k):
        spread(arrived(b, j, k, pos), b, j, k)

    def pick(cond, fn):
        if isinstance(cond, bool):
            if cond:
                fn()
        else:
            pl.when(cond)(fn)

    def relay(ref, b, j, k, origin, way, target):
        part = (slice(None),) * (b == 0) + (pl.ds(way * (rb // 2), rb // 2),)
        send(ref.at[part], b, j, k, origin, way, target, part)

    def serve_ring(b, j, k, dist):
        if dist == half:
            origin = (pos + half) % ring
            send(arrived(b, j, k, origin), b, j, k, origin, 2, sibling)
            return
        pass_on = relay if dist + 1 == half else send
        for way, origin, target in ((0, (pos + ring - dist) % ring, right), (1, (pos + dist) % ring, left)):
            ref = arrived(b, j, k, origin)
            pass_on(ref, b, j, k, origin, way, target)
            send(ref, b, j, k, origin, 2, sibling)

    pieces = ((0, 0), (1, 0), (2, 0), (2, 1), (3, 0), (3, 1))
    order = [(b, j, 0) for b, j in pieces] + [(b, j, k) for b, j in pieces for k in range(1, mp)]
    lag = half + LAG
    served = [0]

    def with_item(t, fn):
        if 0 <= t < len(order):
            fn(*order[t])

    def tick(t):
        with_item(t, lambda b, j, k: k > 0 and serve_column(b, j, k))
        for dist in range(1, half + 1):
            with_item(t - dist - LAG, lambda b, j, k: serve_ring(b, j, k, dist))

    def column_out(p):
        for hop in range(1, mp):
            send_z(*pieces[p], (z + hop) % mp)

    def serve_to(count):
        for t in range(served[0], count):
            for p in PLAN.get(t, ()):
                column_out(p)
            for hop in HID_AT.get(t, ()):
                exchange_in(hid, xh, 0, hop)
            for hop in COT_AT.get(t, ()):
                exchange_in(cot, ct, 1, hop)
            tick(t)
        served[0] = max(served[0], count)

    def whole_at(b, j, k):
        return order.index((b, j, k)) + lag + 1

    def serve_within(i, slots, until):
        first = served[0]
        for slot in range(slots):
            upto = min(until(slot), len(order) + lag)
            if upto > served[0]:
                pl.when(i == slot)(functools.partial(serve_to, upto))
                served[0] = max(served[0], upto)

    def sibling_done(b, j, k):
        zz = (z + mp - k) % mp
        if b == 0:
            ref = wq.at[:, pl.ds(0, width // 2), pl.ds(0, cq)]
        elif b == 1:
            ref = wo.at[pl.ds(0, width // 2), pl.ds(0, cq)]
        else:
            ref = wholes[b].at[pl.ds(0, width // 2), pl.ds(0, hu)]
        pltpu.make_async_copy(ref, ref, sib_sem.at[piece(b, j), zz]).wait()

    def tokens(ref, block):
        return ref.at[pl.ds(pl.multiple_of(block * tok, tok), tok), :]

    def own_local(b):
        zz = z
        rows = pl.ds(pl.multiple_of(d * rb, rb), rb)
        if b == 0:
            dst = wq.at[:, rows, pl.ds(pl.multiple_of(zz * cq, 128), cq)]
        elif b == 1:
            dst = wo.at[rows, pl.ds(pl.multiple_of(zz * cq, 128), cq)]
        else:
            dst = wholes[b].at[rows, pl.ds(pl.multiple_of(zz * cu, 128), cu)]
        return pltpu.make_async_copy(shards[b], dst, local_sem.at[b])

    barrier = pltpu.get_barrier_semaphore()
    def flip(index, bit):
        return index + bit - 2 * bit * ((index // bit) % 2)

    peers = [(d, flip(z, 1 << s)) for s in range(mp.bit_length() - 1)]
    peers += [(flip(d, 1 << s), z) for s in range(1, dp.bit_length() - 1)] + [sibling]
    partners = [sibling, right, left] + [(d, (z + hop) % mp) for hop in range(1, mp)] + peers
    for target in partners:
        pl.semaphore_signal(barrier, inc=1, device_id=target, device_id_type=MESH)
    for b in range(4):
        own_local(b).start()
    own_hid = pltpu.make_async_copy(hid.at[z], tokens(xh, z), local_sem.at[4])
    own_cot = pltpu.make_async_copy(cot.at[z], tokens(ct, z), local_sem.at[5])
    own_hid.start()
    own_cot.start()
    pl.semaphore_wait(barrier, len(partners))

    def exchange_in(src, dst, which, hop):
        there = (z + hop) % mp
        pltpu.make_async_remote_copy(
            src_ref=src.at[there], dst_ref=tokens(dst, z), send_sem=row_send.at[which, there],
            recv_sem=row_recv.at[which, z], device_id=(d, there), device_id_type=MESH,
        ).start()

    def exchange_wait(src, dst, which):
        for hop in range(1, mp):
            there = (z + hop) % mp
            pltpu.make_async_copy(tokens(dst, there), tokens(dst, there), row_recv.at[which, there]).wait()

    def sends_wait(ref, which):
        for hop in range(1, mp):
            there = (z + hop) % mp
            pltpu.make_async_copy(ref, ref, row_send.at[which, there]).wait()

    column_out(0)
    for p, (b, j) in enumerate(pieces):
        start_own(b, j)

    serve_to(PRE_TICKS)
    own_hid.wait()
    exchange_wait(hid, xh, 0)
    length = lens[z]
    separator = seps[z]
    seg0 = seg[0:1, :]
    seg_step = seg[1:2, :] - seg[0:1, :]

    def embed(rows, first):
        at = lax.broadcasted_iota(jnp.int32, (ROWS, 1), 0) + first
        flag = jnp.where(at > separator, 1.0, 0.0).astype(F32)
        return xh[rows, :].astype(F32) + seg0 + flag * seg_step

    @pl.loop(0, seq // ROWS)
    def _(i):
        first = pl.multiple_of(i * ROWS, ROWS)
        rows = pl.ds(first, ROWS)
        low[rows, :] = embed(rows, first).astype(BF16)

    own_local(0).wait()
    tile = 256
    pairs = heads // 2
    lane = lax.broadcasted_iota(jnp.int32, (seq, 2 * HEAD_DIM), 1)

    def half_of(x, hh):
        keep = lane < HEAD_DIM if hh == 0 else lane >= HEAD_DIM
        return jnp.where(keep, x, jnp.zeros_like(x))

    items = 2 * mp

    share = pairs // mp
    spots = mp * (share + 1)

    def attn_until(n):
        paced = PRE_TICKS + (n + 1) * ATTN_TICKS // spots
        return max(paced, whole_at(0, 0, n // (share + 1)))

    def attend(i):
        cols = pl.ds(pl.multiple_of(i * 128, 128), 128)
        q2 = qs[:, cols]
        k2 = ks[:, cols]
        v2t = vs[:, cols].T
        ctxs = []
        for hh in range(2):
            st = dot(half_of(k2, hh), q2, NT)
            valid = lax.broadcasted_iota(jnp.int32, st.shape, 0) < length
            st = jnp.where(valid, st, -1e30)
            e = jnp.exp(st - jnp.max(st, axis=0, keepdims=True))
            p = (e * (1.0 / jnp.sum(e, axis=0, keepdims=True))).astype(BF16)
            probs[2 * i + hh] = p
            ctxs.append(dot(v2t[hh * HEAD_DIM:(hh + 1) * HEAD_DIM], p))
        gctx[:, cols] = jnp.concatenate(ctxs, axis=0).T.astype(BF16)

    @pl.loop(0, spots)
    def _(spot):
        serve_within(spot, spots, attn_until)
        k = spot // (share + 1)
        own = (z + mp - k) % mp

        @pl.when(spot % (share + 1) == 0)
        def _():
            sibling_done(0, 0, k)
            cols = pl.ds(pl.multiple_of(own * cq, 128), cq)
            qs[:, cols] = ((dot(low[...], wq[0, :, cols]) + bias_q[:, cols]) * scale).astype(BF16)
            ks[:, cols] = dot(low[...], wq[1, :, cols]).astype(BF16)
            vs[:, cols] = (dot(low[...], wq[2, :, cols]) + bias_v[:, cols]).astype(BF16)

        @pl.when(spot % (share + 1) > 0)
        def _():
            attend(own * share + spot % (share + 1) - 1)

    own_local(1).wait()
    serve_to(whole_at(1, 0, mp - 1))
    for k in range(mp):
        sibling_done(1, 0, k)

    @pl.loop(0, width // tile)
    def _(i):
        cols = pl.ds(pl.multiple_of(i * tile, tile), tile)
        acc[:, cols] = dot(gctx[...], wo[cols, :], NT)

    @pl.loop(0, seq // ROWS)
    def _(i):
        first = pl.multiple_of(i * ROWS, ROWS)
        rows = pl.ds(first, ROWS)
        x = embed(rows, first) + acc[rows, :] + bias_out[...]
        center = x - row_mean(x)
        inv = lax.rsqrt(row_mean(center * center) + EPS)
        norm = center * inv
        normal[rows, :] = norm
        inverse[rows, :] = jnp.broadcast_to(inv, (ROWS, 128))
        low[rows, :] = (norm * gain_attn[...] + shift_attn[...]).astype(BF16)
        acc[rows, :] = jnp.zeros((ROWS, width), F32)

    own_local(2).wait()
    AFTER_ATTN = served[0]

    def slab(i):
        zz = (z + mp - i % mp) % mp
        return pl.multiple_of(zz * cu + (i // mp) * hu, 128)

    @pl.loop(0, items)
    def _(i):
        serve_within(i, items, lambda n: max(whole_at(2, n // mp, n % mp), AFTER_ATTN + (n + 1) * UP_TICKS // items))
        sibling_done(2, i // mp, i % mp)
        base = slab(i)

        @pl.loop(0, hu // tile)
        def _(n):
            cols = pl.ds(pl.multiple_of(base + n * tile, 128), tile)
            inner = dot(low[...], wu[:, cols]) + expand_bias[:, cols]
            cdf = 0.5 * (1.0 + lax.erf(inner * math.sqrt(0.5)))
            act[:, cols] = (inner * cdf).astype(BF16)
            bell = jnp.exp(-0.5 * inner * inner) * (1.0 / math.sqrt(2.0 * math.pi))
            slope[:, cols] = (cdf + inner * bell).astype(BF16)

    own_local(3).wait()

    @pl.loop(0, items)
    def _(i):
        serve_within(i, items, lambda n: max(whole_at(3, n // mp, n % mp), whole_at(3, 0, mp - 1) + n + 1))
        sibling_done(3, i // mp, i % mp)
        cols = pl.ds(slab(i), hu)

        @pl.loop(0, width // 512)
        def _(n):
            rows = pl.ds(pl.multiple_of(n * 512, 512), 512)
            acc[:, rows] += dot(act[:, cols], wd[rows, cols], NT)

    own_cot.wait()
    exchange_wait(cot, ct, 1)
    early[0] = jnp.zeros(early.shape[1:], F32)
    late[0] = jnp.zeros(late.shape[1:], F32)

    @pl.loop(0, seq // ROWS)
    def _(i):
        rows = pl.ds(pl.multiple_of(i * ROWS, ROWS), ROWS)
        x = normal[rows, :] * gain_attn[...] + shift_attn[...] + acc[rows, :] + bias_down[...]
        center = x - row_mean(x)
        inv = lax.rsqrt(row_mean(center * center) + EPS)
        norm = center * inv
        outb[rows, :] = (norm * gain_ffn[...] + shift_ffn[...]).astype(BF16)
        dy = ct[rows, :].astype(F32)
        e = dy * gain_ffn[...]
        g = inv * (e - row_mean(e) - norm * row_mean(e * norm))
        acc[rows, :] = g
        low[rows, :] = g.astype(BF16)
        early[0, 0:1, :] += jnp.sum(dy, axis=0, keepdims=True)
        early[0, 1:2, :] += jnp.sum(g, axis=0, keepdims=True)

    def push_out(buf, dst, which, there):
        pltpu.make_async_remote_copy(
            src_ref=tokens(buf, there), dst_ref=dst.at[z], send_sem=row_send.at[which, there],
            recv_sem=row_recv.at[which, z], device_id=(d, there), device_id_type=MESH,
        ).start()

    for hop in range(1, mp):
        push_out(outb, out, 2, (z + hop) % mp)
    keep_out = pltpu.make_async_copy(tokens(outb, z), out.at[z], local_sem.at[6])
    keep_out.start()

    wide = 512
    for part in range(units // width):

        @pl.loop(0, width // wide)
        def _(i):
            here = pl.ds(pl.multiple_of(i * wide, wide), wide)
            cols = pl.ds(pl.multiple_of(part * width + i * wide, wide), wide)
            g = (dot(low[...], wd[:, cols]) * slope[:, cols].astype(F32)).astype(BF16)
            act[:, cols] = g
            early[0, 4 + part:5 + part, here] = jnp.sum(g.astype(F32), axis=0, keepdims=True)

    @pl.loop(0, width // wide)
    def _(i):
        cols = pl.ds(pl.multiple_of(i * wide, wide), wide)
        acc[:, cols] += dot(act[...], wu[cols, :], NT)

    @pl.loop(0, seq // ROWS)
    def _(i):
        rows = pl.ds(pl.multiple_of(i * ROWS, ROWS), ROWS)
        g = acc[rows, :]
        norm = normal[rows, :]
        e = g * gain_attn[...]
        first = inverse[rows, 0:1] * (e - row_mean(e) - norm * row_mean(e * norm))
        acc[rows, :] = first
        low[rows, :] = first.astype(BF16)
        early[0, 2:3, :] += jnp.sum(g, axis=0, keepdims=True)
        early[0, 3:4, :] += jnp.sum(first, axis=0, keepdims=True)

    @pl.loop(0, width // wide)
    def _(i):
        cols = pl.ds(pl.multiple_of(i * wide, wide), wide)
        gctx[:, cols] = dot(low[...], wo[:, cols]).astype(BF16)

    def sum_send_step(buf, which, s):
        pltpu.make_async_remote_copy(
            src_ref=buf.at[s], dst_ref=inbox.at[which, s], send_sem=sum_send.at[which, s],
            recv_sem=sum_recv.at[which, s], device_id=peers[s], device_id_type=MESH,
        ).start()

    def sum_take_step(buf, which, s):
        pltpu.make_async_copy(inbox.at[which, s], inbox.at[which, s], sum_recv.at[which, s]).wait()
        buf[s + 1] = buf[s] + inbox[which, s]

    def sum_pass(buf, which, s):
        if s < steps:
            sum_take_step(buf, which, s)
            if s + 1 < steps:
                sum_send_step(buf, which, s + 1)

    steps = len(peers)
    in_loop = min(steps, (pairs - 1) // 2)
    sum_send_step(early, 0, 0)

    @pl.loop(0, pairs)
    def _(i):
        for s in range(in_loop):

            @pl.when(i == 2 * s + 2)
            def _(s=s):
                sum_pass(early, 0, s)

        cols = pl.ds(pl.multiple_of(i * 128, 128), 128)
        q2 = qs[:, cols]
        k2t = ks[:, cols].T
        v2 = vs[:, cols]
        g2 = gctx[:, cols]
        dq, dk, dv = [], [], []
        for hh in range(2):
            p = probs[2 * i + hh]
            pf = p.astype(F32)
            dpt = dot(half_of(v2, hh), g2, NT)
            ds = (pf * (dpt - jnp.sum(pf * dpt, axis=0, keepdims=True))).astype(BF16)
            dk.append(dot(ds, q2))
            dv.append(dot(p, g2))
            dq.append(dot(k2t[hh * HEAD_DIM:(hh + 1) * HEAD_DIM], ds))
        dq2 = jnp.concatenate(dq, axis=0).T.astype(BF16).astype(F32) * scale
        dv2 = jnp.where(lane < HEAD_DIM, dv[0], dv[1]).astype(BF16)
        qs[:, cols] = dq2.astype(BF16)
        ks[:, cols] = jnp.where(lane < HEAD_DIM, dk[0], dk[1]).astype(BF16)
        vs[:, cols] = dv2
        late[0, 0:1, cols] = jnp.sum(dq2, axis=0, keepdims=True)
        late[0, 1:2, cols] = jnp.sum(dv2.astype(F32), axis=0, keepdims=True)

    sum_send_step(late, 1, 0)
    side = seq // 2
    per = mp // 2
    mine = z // per
    for turn in range(2):
        block = 1 - mine if turn == 0 else mine
        rows = pl.ds(pl.multiple_of(block * side, side), side)

        @pl.loop(0, width // wide)
        def _(i):
            cols = pl.ds(pl.multiple_of(i * wide, wide), wide)
            x = acc[rows, cols]
            x += dot(qs[rows, :], wq[0, cols, :], NT)
            x += dot(ks[rows, :], wq[1, cols, :], NT)
            x += dot(vs[rows, :], wq[2, cols, :], NT)
            xh[rows, cols] = x.astype(BF16)

        sum_pass(early, 0, in_loop + turn)
        sum_pass(late, 1, turn)
        for q in range(per):
            there = block * per + (z + q + turn) % per
            if turn == 0 or q < per - 1:
                push_out(xh, grad, 3, there)
    keep_grad = pltpu.make_async_copy(tokens(xh, z), grad.at[z], local_sem.at[7])
    keep_grad.start()

    for s in range(2, steps):
        sum_pass(early, 0, in_loop + s)
        sum_pass(late, 1, s)
    sums[0] = early[steps]
    sums[1] = late[steps]
    for which, buf in ((0, early), (1, late)):
        for s in range(steps):
            pltpu.make_async_copy(buf.at[s], buf.at[s], sum_send.at[which, s]).wait()

    keep_out.wait()
    keep_grad.wait()
    for which, src in ((0, tokens(xh, z)), (1, tokens(xh, z)), (2, tokens(xh, z)), (3, tokens(xh, z))):
        sends_wait(src, which)
    for which, ref in ((2, out), (3, grad)):
        for hop in range(1, mp):
            there = (z + hop) % mp
            pltpu.make_async_copy(ref.at[there], ref.at[there], row_recv.at[which, there]).wait()
    for b in range(4):
        ref = wholes[b]
        cols = (cq if b < 2 else cu) * mp
        ways = (
            (rb * (2 * half - 1), cols // 2),
            (rb * (2 * half - 1), cols // 2),
            (width // 2, cols),
            (rb, cols - cols // mp),
        )
        for way, (r, c) in enumerate(ways):
            part = ref.at[:, pl.ds(0, r), pl.ds(0, c)] if b == 0 else ref.at[pl.ds(0, r), pl.ds(0, c)]
            pltpu.make_async_copy(part, part, send_sem.at[b, way]).wait()


def on_device(
    hidden_in, lengths, separators, seg_table, query_key_value_weight, output_weight, up_weight, down_weight,
    bias_q, bias_v, bias_out, expand_bias, bias_down, gain_attn, shift_attn, gain_ffn, shift_ffn, cotangent,
):
    dp, mp = lax.axis_size("dp"), lax.axis_size("mp")
    here, tok, width = hidden_in.shape
    assert here == mp
    seq = tok * mp
    units = up_weight.shape[1] * mp
    heads = width // HEAD_DIM
    vmem = pl.BlockSpec(memory_space=pltpu.VMEM)
    smem = pl.BlockSpec(memory_space=pltpu.SMEM)
    anys = pl.BlockSpec(memory_space=pl.ANY)
    rows = [seg_table] + [
        v.reshape(1, -1)
        for v in (bias_q, bias_v, bias_out, expand_bias, bias_down, gain_attn, shift_attn, gain_ffn, shift_ffn)
    ]
    steps = dp.bit_length() + mp.bit_length() - 2
    summed = (4 + units // width, width)
    moved = jax.ShapeDtypeStruct(hidden_in.shape, BF16)
    ring = dp // 2
    sem = pltpu.SemaphoreType.DMA
    results = pl.pallas_call(
        functools.partial(step_kernel, (dp, mp, seq, width, units)),
        name="step",
        out_shape=(moved, moved, jax.ShapeDtypeStruct((2,) + summed, F32)),
        in_specs=[smem, smem] + [vmem] * 10 + [anys] * 6,
        out_specs=(anys, anys, vmem),
        scratch_shapes=[
            pltpu.VMEM((3, width, width), BF16),
            pltpu.VMEM((width, width), BF16),
            pltpu.VMEM((width, units), BF16),
            pltpu.VMEM((width, units), BF16),
            *[pltpu.VMEM((seq, width), BF16)] * 7,
            pltpu.VMEM((heads, seq, seq), BF16),
            pltpu.VMEM((seq, width), F32),
            pltpu.VMEM((seq, 128), F32),
            pltpu.VMEM((seq, width), F32),
            pltpu.VMEM((seq, units), BF16),
            pltpu.VMEM((seq, units), BF16),
            pltpu.VMEM((seq, width), BF16),
            pltpu.VMEM((steps + 1,) + summed, F32),
            pltpu.VMEM((steps + 1,) + summed, F32),
            pltpu.VMEM((2, steps) + summed, F32),
            sem((8,)),
            sem((6, mp, ring)),
            sem((6, mp)),
            sem((4, 4)),
            sem((4, mp)),
            sem((4, mp)),
            sem((2, steps)),
            sem((2, steps)),
        ],
        compiler_params=pltpu.CompilerParams(collective_id=0, has_side_effects=True, vmem_limit_bytes=67043328),
    )(
        lengths, separators, *rows, hidden_in, cotangent, jnp.swapaxes(query_key_value_weight, 0, 1),
        output_weight, up_weight, down_weight,
    )
    sums = results[2] * (1.0 / (here * seq * dp))
    first, last = sums[0], sums[1]
    return results[:2] + (last[0], last[1], first[3], first[4:].reshape(-1), first[1], first[2], first[0])


def solution(mesh):
    rows = P("dp", "mp", None)
    frozen = P("dp", "mp")
    placed = (rows, P("dp"), P("dp"), P(), P("dp", None, "mp"), frozen, frozen, frozen) + (P(),) * 9 + (rows,)
    return jax.shard_map(on_device, mesh=mesh, in_specs=placed, out_specs=(rows, rows) + (P(),) * 7, check_vma=False)
```
